32 devices in a mesh: morton: 32 (over z, y, x, core).
Axes of the slice: x: 2, y: 2, z: 4, core: 2. Of those that a mesh axis runs over, the one named last changes fastest.
Arguments:
- offsets: float32 [3, 262144], P(None, 'morton'), may hold values from -0.5 to 0.5
- forces: float32 [3, 262144], P(None, 'morton'), may hold values from -6 to 6
- counts: int32 [2048], P('morton'), may hold values from 1 to 128
- uc2ue: float32 [456, 456], replicated, may hold values from -0.25 to 0.25
- m2m_ops: float32 [8, 456, 456], replicated, may hold values from -0.09375 to 0.09375
- compress: float32 [456, 64], replicated, may hold values from -0.25 to 0.25
- m2l_ops: bfloat16 [316, 64, 64], replicated, may hold values from -0.0546875 to 0.0546875
- root_ops: bfloat16 [7, 64, 64], replicated, may hold values from -0.375 to 0.375
Outputs:
- local_boxes: float32 [2336, 64], P('morton')
- local_roots: float32 [4, 64], replicated
The draws below stay inside these ranges and needn't reach their ends.
Inputs may be any that keep to these rules, and one draw needn't show every extreme that they name: The live points of a leaf are its first counts slots; later slots belong to no point.
All inputs are finite; a program needn't handle non-finite values.
Results may differ from the reference program's by a relative error of at most 0.0031.
Values may be sent and summed in bfloat16 or wider, within the bound.
A program may use at most 192 MiB of HBM per device.

```python
import jax
import jax.numpy as jnp
import numpy as np
from jax import lax

SURF_ORDER = 6
NCOEF = 456
RANK = 64
LEVELS = 2
P_CAP = 128
NDIR = 316
SIDE = 4
LEAF_DEV = 64
BOX_DEV = 73
NROOT = 4
LEAVES = 2048
POINT_SLOT_TOTAL = 262144
N_MORTON = 32


def set_ends(values, stream_key, low, largest):
    shape = values.shape
    index_at = [jax.random.randint(jax.random.fold_in(stream_key, axis), (), 0, shape[axis]) for axis in range(len(shape))]
    values = values.at[tuple(index_at)].set(low)
    longest = shape.index(max(shape))
    index_at[longest] = (index_at[longest] + 1) % shape[longest]
    return values.at[tuple(index_at)].set(largest)


def level_of(rng, dims, cuts, least, high):
    gain, own = 1.0, jax.random.fold_in(rng, 6)
    for dim, parts in cuts:
        draws = jnp.exp(jax.random.uniform(jax.random.fold_in(own, dim), (parts,), jnp.float32, least / len(cuts), high / len(cuts)))
        gain = gain * jnp.repeat(draws, dims[dim] // parts).reshape([-1 if axis == dim else 1 for axis in range(len(dims))])
    return gain


def bell_draw(own_key, shape, deviation, reach, split=(), held_as=jnp.bfloat16):
    drawn = jax.random.normal(own_key, shape, jnp.float32) * deviation
    if len(split) > 0:
        drawn = level_of(own_key, shape, split, -0.22, 0.18) * drawn
    return jnp.clip(drawn, min=-reach, max=reach).astype(held_as)


def setup_inputs(seed: int = 0) -> dict:
    key_list = jax.random.split(jax.random.key(seed), 9)
    offsets = jnp.clip(jax.random.uniform(key_list[0], (3, POINT_SLOT_TOTAL), jnp.float32, -0.5, 0.5) * level_of(key_list[0], (3, POINT_SLOT_TOTAL), ((1, 32),), -0.4, 0.0), -0.5, 0.5)
    forces = bell_draw(key_list[1], (3, POINT_SLOT_TOTAL), 1.0, 6.0, ((1, 32),), jnp.float32)
    counts = set_ends(jax.random.randint(key_list[2], (LEAVES,), 1, P_CAP + 1), jax.random.fold_in(key_list[2], 1), 1, P_CAP).astype(jnp.int32)
    uc2ue = bell_draw(key_list[3], (NCOEF, NCOEF), NCOEF ** -0.5, 0.25, (), jnp.float32)
    m2m_ops = bell_draw(key_list[4], (8, NCOEF, NCOEF), (8 * NCOEF) ** -0.5, 0.09375, (), jnp.float32)
    compress = bell_draw(key_list[5], (NCOEF, RANK), NCOEF ** -0.5, 0.25, (), jnp.float32)
    m2l_ops = bell_draw(key_list[6], (NDIR, RANK, RANK), (189 * RANK) ** -0.5, 0.0546875)
    root_ops = bell_draw(key_list[7], (2 * NROOT - 1, RANK, RANK), (RANK * (N_MORTON // 8)) ** -0.5, 0.375)
    return dict(offsets=offsets, forces=forces, counts=counts, uc2ue=uc2ue, m2m_ops=m2m_ops, compress=compress, m2l_ops=m2l_ops, root_ops=root_ops)


precise = lax.Precision.HIGHEST
check_radius = 1.475

def surface_points():
    tick_values = np.linspace(-1.0, 1.0, SURF_ORDER)
    chosen = []
    for along_x in range(SURF_ORDER):
        for along_y in range(SURF_ORDER):
            for along_z in range(SURF_ORDER):
                if min(along_x, along_y, along_z) == 0 or max(along_x, along_y, along_z) == SURF_ORDER - 1:
                    chosen.append((tick_values[along_x], tick_values[along_y], tick_values[along_z]))
    return check_radius * np.array(chosen).T

def direction_lookup():
    direction_list = []
    for step_x in range(-3, 4):
        for step_y in range(-3, 4):
            for step_z in range(-3, 4):
                if max(abs(step_x), abs(step_y), abs(step_z)) >= 2:
                    direction_list.append((step_x, step_y, step_z))
    lookup = {}
    for position, entry in enumerate(direction_list):
        lookup[entry] = position
    index_table = np.full((216, 8), len(direction_list), dtype=np.int32)
    for along_x in range(6):
        for along_y in range(6):
            for along_z in range(6):
                for oddness_along_x in range(2):
                    for parity_y in range(2):
                        for oddness_along_z in range(2):
                            entry = (along_x - 2 - oddness_along_x, along_y - 2 - parity_y, along_z - 2 - oddness_along_z)
                            if entry in lookup:
                                index_table[(along_x * 6 + along_y) * 6 + along_z, (oddness_along_x * 2 + parity_y) * 2 + oddness_along_z] = lookup[entry]
    return index_table

def leaf_potentials(offsets, forces, counts):
    slot_ids = lax.broadcasted_iota(jnp.int32, (counts.shape[0], P_CAP), 1)
    live_mask = (slot_ids < counts[:, None]).astype(jnp.float32)
    masked = forces * live_mask[None]
    targets = jnp.asarray(surface_points(), dtype=jnp.float32)
    separation = targets[:, None, None, :] - offsets[..., None]
    inverse = lax.rsqrt(lax.optimization_barrier(jnp.sum(separation * separation, axis=0)))
    projected_values = lax.optimization_barrier(jnp.sum(separation * masked[..., None], axis=0))
    velocity = masked[..., None] * inverse[None] + separation * (projected_values * inverse * inverse * inverse)[None]
    total_sum = lax.optimization_barrier(jnp.sum(velocity, axis=2))
    return jnp.transpose(total_sum, (1, 0, 2)).reshape(counts.shape[0], NCOEF)

def merge_children(density, m2m_ops):
    half_side = density.shape[0] // 2
    children = density.reshape(half_side, 2, half_side, 2, half_side, 2, NCOEF)
    octants = m2m_ops.reshape(2, 2, 2, NCOEF, NCOEF)
    return jnp.einsum('apbqcrx,pqrxy->abcy', children, octants, precision=precise)

def upward_tree(offsets, forces, counts, uc2ue, m2m_ops):
    check = leaf_potentials(offsets.reshape(3, LEAF_DEV, P_CAP), forces.reshape(3, LEAF_DEV, P_CAP), counts)
    density = jnp.dot(check, uc2ue, precision=precise, preferred_element_type=jnp.float32)
    density = density.reshape(SIDE, SIDE, SIDE, NCOEF)
    levels = [density]
    for level_id in range(LEVELS):
        density = merge_children(density, m2m_ops)
        levels.insert(0, density)
    return levels

def shrink(density, compress):
    return jnp.dot(density, compress, precision=precise, preferred_element_type=jnp.float32).astype(jnp.bfloat16)

def interaction_matrix(m2l_ops):
    padded_ops = jnp.concatenate([m2l_ops, jnp.zeros((1, RANK, RANK), m2l_ops.dtype)], axis=0)
    picked = padded_ops[jnp.asarray(direction_lookup())]
    return jnp.transpose(picked, (0, 2, 1, 3)).reshape(216 * RANK, 8 * RANK)

def neighbourhood(window):
    gathered = window
    for axis_number in range(3):
        count_here = (gathered.shape[axis_number] - 4) // 2
        pieces = [lax.slice_in_dim(gathered, start_offset, start_offset + 2 * count_here - 1, 2, axis_number) for start_offset in range(6)]
        gathered = jnp.stack(pieces, axis=-2)
    parents = gathered.shape[0] * gathered.shape[1] * gathered.shape[2]
    return gathered.reshape(parents, 216 * RANK)

def spread_children(products, parent_shape):
    arranged = products.reshape(parent_shape[0], parent_shape[1], parent_shape[2], 2, 2, 2, RANK)
    arranged = jnp.transpose(arranged, (0, 3, 1, 4, 2, 5, 6))
    return arranged.reshape(2 * parent_shape[0], 2 * parent_shape[1], 2 * parent_shape[2], RANK)

def to_grid(stacked, side_boxes):
    columns_x = N_MORTON // 4
    arranged = stacked.reshape(columns_x, 2, 2, side_boxes, side_boxes, side_boxes, RANK)
    arranged = jnp.transpose(arranged, (0, 3, 1, 4, 2, 5, 6))
    return arranged.reshape(columns_x * side_boxes, 2 * side_boxes, 2 * side_boxes, RANK)

def from_grid(grid_values, side_boxes):
    columns_x = N_MORTON // 4
    arranged = grid_values.reshape(columns_x, side_boxes, 2, side_boxes, 2, side_boxes, RANK)
    arranged = jnp.transpose(arranged, (0, 2, 4, 1, 3, 5, 6))
    return arranged.reshape(N_MORTON, side_boxes * side_boxes * side_boxes, RANK)

def level_locals(multipole_grid, weights):
    cross_side = multipole_grid.shape[1]
    padded = jnp.pad(multipole_grid, ((2, 2), (2, 2), (2, 2), (0, 0))).astype(jnp.float32)

    def one_root(root_id):
        window = lax.dynamic_slice_in_dim(padded, root_id * cross_side, cross_side + 4, 0)
        products = jnp.dot(neighbourhood(window), weights, precision=precise)
        half_side = cross_side // 2
        return spread_children(products, (half_side, half_side, half_side))
    blocks = lax.map(one_root, jnp.arange(NROOT, dtype=jnp.int32))
    return blocks.reshape(NROOT * cross_side, cross_side, cross_side, RANK)

def root_locals(root_multipoles, root_ops):
    blank = jnp.zeros((NROOT, RANK), jnp.float32)
    padded = jnp.concatenate([blank, root_multipoles.astype(jnp.float32), blank], axis=0)

    def accumulate(step_index, running):
        distance = (step_index - (NROOT - 1)).astype(jnp.int32)
        source = lax.dynamic_slice_in_dim(padded, (NROOT + distance).astype(jnp.int32), NROOT, 0)
        weight = jnp.where(jnp.abs(distance) >= 2, 1.0, 0.0).astype(jnp.float32)
        root_matrix = root_ops[step_index].astype(jnp.float32)
        return running + weight * jnp.dot(source, root_matrix, precision=precise)
    return lax.fori_loop(0, 2 * NROOT - 1, accumulate, jnp.zeros((NROOT, RANK), jnp.float32))

def reference(offsets, forces, counts, uc2ue, m2m_ops, compress, m2l_ops, root_ops):
    split_offsets = jnp.transpose(offsets.reshape(3, N_MORTON, LEAF_DEV * P_CAP), (1, 0, 2))
    split_forces = jnp.transpose(forces.reshape(3, N_MORTON, LEAF_DEV * P_CAP), (1, 0, 2))
    split_counts = counts.reshape(N_MORTON, LEAF_DEV)

    def device_pass(inputs):
        levels = upward_tree(inputs[0], inputs[1], inputs[2], uc2ue, m2m_ops)
        multipoles = tuple((shrink(level_values, compress) for level_values in levels))
        return (multipoles, levels[0].reshape(NCOEF))
    multipoles, device_density = lax.map(device_pass, (split_offsets, split_forces, split_counts))
    weights = interaction_matrix(m2l_ops).astype(jnp.float32)
    level_count = []
    for level_id in range(LEVELS + 1):
        side_boxes = 2 ** level_id
        grid_values = level_locals(to_grid(multipoles[level_id], side_boxes), weights)
        level_count.append(from_grid(grid_values, side_boxes))
    local_boxes = jnp.concatenate(level_count, axis=1).reshape(N_MORTON * BOX_DEV, RANK)
    octants = m2m_ops.reshape(2, 2, 2, NCOEF, NCOEF)
    root_density = jnp.einsum('rpqsx,pqsxy->ry', device_density.reshape(NROOT, 2, 2, 2, NCOEF), octants, precision=precise)
    local_roots = root_locals(shrink(root_density, compress), root_ops)
    return (local_boxes, local_roots)
```

```python
import functools

import jax
import jax.numpy as jnp
import numpy as np
from jax import lax
from jax.experimental import pallas as pl
from jax.experimental.pallas import tpu as pltpu
from jax.sharding import PartitionSpec as P

SURF_ORDER = 6
NCOEF = 456
RANK = 64
P_CAP = 128
LEAF_DEV = 64
HALF = RANK // 2
PITCH = HALF + 8


check_radius = 1.475
MESH = pl.DeviceIdType.MESH


def surface_points():
    tick_values = np.linspace(-1.0, 1.0, SURF_ORDER)
    chosen = []
    for along_x in range(SURF_ORDER):
        for along_y in range(SURF_ORDER):
            for along_z in range(SURF_ORDER):
                if (
                    min(along_x, along_y, along_z) == 0
                    or max(along_x, along_y, along_z) == SURF_ORDER - 1
                ):
                    chosen.append(
                        (tick_values[along_x], tick_values[along_y], tick_values[along_z])
                    )
    return check_radius * np.array(chosen).T


def two_parts(value):
    high = value.astype(jnp.bfloat16).astype(jnp.float32)
    return high, value - high


def product(value, high, low, contracted=0):
    rows = value.shape[0]
    parts = jnp.concatenate(two_parts(value), axis=0).astype(jnp.bfloat16)
    dims = (((1,), (contracted,)), ((), ()))
    both = lax.dot_general(parts, low, dims, preferred_element_type=jnp.float32)
    both += lax.dot_general(parts, high, dims, preferred_element_type=jnp.float32)
    return both[:rows] + both[rows:]


def halves(matrix):
    high, low = two_parts(matrix)
    return high.astype(jnp.bfloat16), low.astype(jnp.bfloat16)


def upward_kernel(counts_ref, offsets_ref, forces_ref, targets_ref, uc2ue_ref, compress_ref, m2m_hbm,
                  small_ref, block_ref, m2m, m2m_high, m2m_low, check, arrivals):
    f32, bf16 = jnp.float32, jnp.bfloat16
    points = NCOEF // 3
    octant = lax.axis_index("morton") % 8
    for o in range(8):
        pltpu.make_async_copy(m2m_hbm.at[o], m2m.at[o], arrivals.at[o]).start()
    check[...] = jnp.zeros_like(check)
    lane = lax.broadcasted_iota(jnp.int32, (8, 128), 1)
    lane_row = lax.broadcasted_iota(jnp.int32, (1, 128), 1)

    def one_leaf(leaf, carry):
        odd = (leaf >> 4 & 1) * 4 + (leaf >> 2 & 1) * 2 + (leaf & 1)
        parent = (leaf >> 5 & 1) * 4 + (leaf >> 3 & 1) * 2 + (leaf >> 1 & 1)
        here = lane == odd * 8 + parent
        slots = pl.ds(pl.multiple_of(leaf * P_CAP, P_CAP), P_CAP)
        live = lane_row < counts_ref[leaf]
        place = [jnp.broadcast_to(offsets_ref[s : s + 1, slots], (8, P_CAP)) for s in range(3)]
        force = [
            jnp.broadcast_to(jnp.where(live, forces_ref[s : s + 1, slots], 0.0), (8, P_CAP))
            for s in range(3)
        ]
        for first in range(0, points, 8):
            apart = [targets_ref[s * points + first : s * points + first + 8] - place[s] for s in range(3)]
            inverse = lax.rsqrt(apart[0] * apart[0] + apart[1] * apart[1] + apart[2] * apart[2])
            projected = apart[0] * force[0] + apart[1] * force[1] + apart[2] * force[2]
            scaled = projected * inverse * inverse
            for s in range(3):
                value = (force[s] + apart[s] * scaled) * inverse
                summed = jnp.sum(value, axis=1, keepdims=True)
                rows = slice(s * points + first, s * points + first + 8)
                check[rows] = jnp.where(here, summed, check[rows])
        return carry

    lax.fori_loop(0, LEAF_DEV, one_leaf, 0, unroll=2)

    potentials = jnp.transpose(check[...])[:LEAF_DEV, :NCOEF]
    leaf_density = product(potentials, *halves(uc2ue_ref[...]))
    mid_density = jnp.zeros((8, NCOEF), f32)
    for o in range(8):
        pltpu.make_async_copy(m2m_hbm.at[o], m2m.at[o], arrivals.at[o]).wait()
        high, low = halves(m2m[o])
        m2m_high[o] = high
        m2m_low[o] = low
        mid_density += product(leaf_density[8 * o : 8 * o + 8], high, low)
    own_density = jnp.zeros((8, NCOEF), f32)
    for o in range(8):
        child = jnp.broadcast_to(mid_density[o : o + 1], (8, NCOEF))
        own_density += product(child, m2m_high[o], m2m_low[o])
    lifted = product(own_density, m2m_high[octant], m2m_low[octant])
    stacked = jnp.concatenate([leaf_density, mid_density, own_density, lifted], axis=0)
    shrunk = product(stacked, *halves(compress_ref[...]), contracted=1)
    rounded = shrunk[:80].astype(bf16)
    row = lax.broadcasted_iota(jnp.int32, (80, 80), 0)
    col = lax.broadcasted_iota(jnp.int32, (80, 80), 1)
    odd = (row >> 4 & 1) * 4 + (row >> 2 & 1) * 2 + (row & 1)
    parent = (row >> 5 & 1) * 4 + (row >> 3 & 1) * 2 + (row >> 1 & 1)
    wanted = jnp.where(row < LEAF_DEV, odd * 8 + parent, row)
    ordered = jnp.dot(jnp.where(col == wanted, 1.0, 0.0).astype(bf16), rounded, preferred_element_type=f32)
    block_ref[...] = jnp.concatenate([ordered, ordered], axis=1).astype(bf16)
    small_ref[...] = jnp.concatenate([rounded.astype(f32)[72:80], shrunk[80:88]], axis=1)


def upward(offsets, forces, counts, uc2ue, m2m_ops, compress):
    vmem = pl.BlockSpec(memory_space=pltpu.VMEM)
    targets = np.repeat(surface_points().reshape(NCOEF, 1), P_CAP, axis=1)
    return pl.pallas_call(
        upward_kernel,
        out_shape=(
            jax.ShapeDtypeStruct((8, 128), jnp.float32),
            jax.ShapeDtypeStruct((80, 128), jnp.bfloat16),
        ),
        in_specs=[pl.BlockSpec(memory_space=pltpu.SMEM)] + [vmem] * 5 + [pl.BlockSpec(memory_space=pl.ANY)],
        out_specs=(vmem, vmem),
        scratch_shapes=[
            pltpu.VMEM(m2m_ops.shape, jnp.float32),
            pltpu.VMEM(m2m_ops.shape, jnp.bfloat16),
            pltpu.VMEM(m2m_ops.shape, jnp.bfloat16),
            pltpu.VMEM((512, 128), jnp.float32),
            pltpu.SemaphoreType.DMA((8,)),
        ],
    )(counts, offsets, forces, jnp.asarray(targets, dtype=jnp.float32), uc2ue, compress.T, m2m_ops)


def exchange_kernel(peers, small_ref, block_ref, stored_ref, root_ref, boxes_ref, roots_ref,
                    every, nearby, leaf_rows, mid_rows, operator_rows, padded, send_all, recv_all, send_near, recv_near):
    f32, bf16 = jnp.float32, jnp.bfloat16
    me = lax.axis_index("morton")
    columns_x, root_count = peers // 4, peers // 8
    column, y_bit, z_bit = me // 4, me // 2 % 2, me % 2
    own = me % 4
    barrier = pltpu.get_barrier_semaphore()

    def greet(k, carry):
        pl.semaphore_signal(barrier, inc=1, device_id=((me + k) % peers,), device_id_type=MESH)
        return carry

    lax.fori_loop(1, peers, greet, 0)

    def near_copy(number, arriving=False):
        dc, flip_y, flip_z = number // 4 - 1, number // 2 % 2, number % 2
        other = (y_bit + flip_y) % 2 * 2 + (z_bit + flip_z) % 2
        peer = (column + dc + columns_x) % columns_x * 4 + other
        return pltpu.make_async_remote_copy(
            src_ref=block_ref, dst_ref=nearby.at[1 - dc, other if arriving else own],
            send_sem=send_near.at[number], recv_sem=recv_near.at[number],
            device_id=(peer,), device_id_type=MESH)

    def small_copy(k, slot):
        return pltpu.make_async_remote_copy(
            src_ref=small_ref, dst_ref=every.at[slot], send_sem=send_all.at[k],
            recv_sem=recv_all.at[k], device_id=((me + k) % peers,), device_id_type=MESH)

    row = lax.broadcasted_iota(jnp.int32, (224, 256), 0)
    col = lax.broadcasted_iota(jnp.int32, (224, 256), 1)
    step_y = (row >> 5) - 3
    slot = ((row >> 4) & 1) * 4 + (col >> 6)
    step_z = jnp.where(slot < 4, slot - 3 + 3 * (slot >> 1), slot - 5)
    usable = slot < 7

    def chosen(side_bits, target, source, step, bit):
        target = (bit << side_bits) + target
        return (source - target == step) & (jnp.abs((source >> 1) - (target >> 1)) <= 1)

    leaf_select = (
        usable
        & chosen(2, (row >> 2) & 3, (((col >> 5) & 1) << 2) + ((col >> 2) & 3), step_y, y_bit)
        & chosen(2, row & 3, (((col >> 4) & 1) << 2) + (col & 3), step_z, z_bit)
    )
    leaf_select = jnp.where(leaf_select, 1.0, 0.0).astype(bf16)
    mid_base = (
        usable
        & ((row & 15) < 4)
        & ((col & 15) < 8)
        & chosen(1, (row >> 1) & 1, (((col >> 5) & 1) << 1) + ((col >> 1) & 1), step_y, y_bit)
        & chosen(1, row & 1, (((col >> 4) & 1) << 1) + (col & 1), step_z, z_bit)
    )
    mid_select = [
        jnp.where(mid_base & (((col >> 2) & 1) == lx), 1.0, 0.0).astype(bf16) for lx in range(2)
    ]
    on_diagonal = (lax.broadcasted_iota(jnp.int32, (256, 256), 0) >> 6) == (
        (lax.broadcasted_iota(jnp.int32, (256, 256), 1) >> 5) & 3
    )

    blank = jnp.zeros((14, 16, 256), bf16)
    leaf_rows[0] = blank
    leaf_rows[9] = blank
    mid_rows[0] = blank
    mid_rows[7] = blank

    pl.semaphore_wait(barrier, peers - 1)
    near_numbers = [number for number in range(12) if number != 4]
    for number in near_numbers:
        near_copy(number).start()

    def send_small(k, carry):
        small_copy(k, me).start()
        return carry

    lax.fori_loop(1, peers, send_small, 0)
    every[me] = small_ref[...]
    nearby[1, own] = block_ref[...]

    directions = stored_ref.shape[2]

    def turn(j, carry):
        pairs = jnp.concatenate([stored_ref[j], stored_ref[j + HALF]], axis=0)
        operator_rows[pl.ds(j, directions, stride=PITCH), :] = jnp.transpose(pairs).astype(f32)
        return carry

    lax.fori_loop(0, HALF, turn, 0, unroll=4)

    for number in near_numbers:
        near_copy(number, True).wait_recv()

    for c in range(3):
        inside = (column + c >= 1) & (column + c <= columns_x)
        diagonal = jnp.where(on_diagonal & inside, 1.0, 0.0).astype(bf16)

        def spread(first):
            stack = nearby[c, :, first : first + 16, :].reshape(64, 128)
            low, high = stack[:, :HALF], stack[:, HALF:RANK]
            wide = jnp.concatenate([low] * 4 + [high] * 4, axis=1)
            return jnp.concatenate([wide] * 4, axis=0) * diagonal

        for lx in range(4):
            plane = 4 * c + lx - 4
            if -2 <= plane <= 5:
                got = jnp.dot(leaf_select, spread(16 * lx), preferred_element_type=f32)
                leaf_rows[plane + 3] = got.astype(bf16).reshape(14, 16, 256)
        sources = spread(64)
        for lx in range(2):
            plane = 2 * c + lx - 2
            got = jnp.dot(mid_select[lx], sources, preferred_element_type=f32)
            mid_rows[plane + 3] = got.astype(bf16).reshape(14, 16, 256)

    bases = {-3: 0, -2: 49, 2: 218, 3: 267}
    first_direction = 0
    odd_target = (lax.broadcasted_iota(jnp.int32, (192, 128), 0) >> 4) & 1
    total = jnp.zeros((192, 128), f32)
    for u in range(7):
        part = jnp.zeros((192, 128), f32)
        for v in range(7):

            def operand(quads):
                rows = []
                for lanes in (slice(0, 128), slice(128, 256)):
                    for ref, count in ((leaf_rows, 4), (mid_rows, 2)):
                        pieces = [
                            ref[u : u + count, 2 * v + quad, :, lanes].reshape(16 * count, 128)
                            for quad in quads
                        ]
                        rows.append(jnp.concatenate(pieces, axis=1))
                return jnp.concatenate(rows, axis=0)

            def operators(steps):
                rows = [operator_rows[(first_direction + k) * PITCH : (first_direction + k) * PITCH + HALF] for k in steps]
                return jnp.concatenate(rows, axis=0).astype(bf16)

            if 2 <= u <= 4 and 2 <= v <= 4:
                part += jnp.dot(operand((0,)), operators((0, 1, 2, 3)), preferred_element_type=f32)
                first_direction += 4
            else:
                part += jnp.dot(operand((0, 1)), operators((0, 1, 5, 6, 2, 3, 4, 4)), preferred_element_type=f32)
                first_direction += 7
        if u == 0:
            part = jnp.where(odd_target == 1, part, 0.0)
        if u == 6:
            part = jnp.where(odd_target == 0, part, 0.0)
        total += part
    total = total[:96, :RANK] + total[96:, RANK:]
    boxes_ref[1:5] = total[64:68]
    boxes_ref[5:9] = total[80:84]
    boxes_ref[9:73] = total[:64]

    def small_arrived(k, carry):
        small_copy(k, (me - k + peers) % peers).wait_recv()
        return carry

    lax.fori_loop(1, peers, small_arrived, 0)

    own_total = jnp.zeros((8, RANK), f32)
    for u in (-3, -2, 2, 3):
        other = column + u
        good = (other >= 0) & (other < columns_x)
        if u == -3:
            good = good & (column % 2 == 1)
        if u == 3:
            good = good & (column % 2 == 0)
        wrapped = (other + 4 * columns_x) % columns_x
        part = jnp.zeros((8, RANK), f32)
        for sy in range(2):
            for sz in range(2):
                direction = bases[u] + (sy - y_bit + 3) * 7 + (sz - z_bit + 3)
                source = every[wrapped * 4 + sy * 2 + sz].astype(bf16)
                rows = pl.ds(pl.multiple_of(direction * PITCH, 8), HALF)
                operator = operator_rows[rows].astype(bf16)
                part += jnp.dot(source[:, :HALF], operator[:, :RANK], preferred_element_type=f32)
                part += jnp.dot(source[:, HALF:RANK], operator[:, RANK:], preferred_element_type=f32)
        own_total += jnp.where(good, part, 0.0)
    boxes_ref[0:1] = own_total[:1]

    padded[...] = jnp.zeros_like(padded)
    for r in range(root_count):
        grouped = jnp.sum(every[8 * r : 8 * r + 8], axis=0)
        padded[root_count + r : root_count + r + 1] = grouped[:1]
    found = jnp.zeros((root_count, RANK), f32)
    for k in range(2 * root_count - 1):
        distance = k - (root_count - 1)
        if abs(distance) >= 2:
            start = root_count + distance
            source = padded[start : start + root_count, :][:, RANK:].astype(bf16)
            found += jnp.dot(source, root_ref[k], preferred_element_type=f32)
    roots_ref[...] = found

    for number in near_numbers:
        near_copy(number).wait_send()

    def small_sent(k, carry):
        small_copy(k, me).wait_send()
        return carry

    lax.fori_loop(1, peers, small_sent, 0)


def far_field(small, block, m2l_ops, root_ops):
    peers = lax.axis_size("morton")
    root_count = peers // 8
    vmem = pl.BlockSpec(memory_space=pltpu.VMEM)
    return pl.pallas_call(
        functools.partial(exchange_kernel, peers),
        out_shape=(
            jax.ShapeDtypeStruct((LEAF_DEV + 9, RANK), jnp.float32),
            jax.ShapeDtypeStruct((root_count, RANK), jnp.float32),
        ),
        in_specs=[vmem] * 4,
        out_specs=(vmem,) * 2,
        scratch_shapes=[
            pltpu.VMEM((peers, 8, 128), jnp.float32),
            pltpu.VMEM((3, 4, 80, 128), jnp.bfloat16),
            pltpu.VMEM((10, 14, 16, 256), jnp.bfloat16),
            pltpu.VMEM((8, 14, 16, 256), jnp.bfloat16),
            pltpu.VMEM((m2l_ops.shape[0] * PITCH, 2 * RANK), jnp.float32),
            pltpu.VMEM((3 * root_count, 128), jnp.float32),
            pltpu.SemaphoreType.DMA((peers,)),
            pltpu.SemaphoreType.DMA((peers,)),
            pltpu.SemaphoreType.DMA((12,)),
            pltpu.SemaphoreType.DMA((12,)),
        ],
        compiler_params=pltpu.CompilerParams(collective_id=0, has_side_effects=True),
    )(small, block, jnp.transpose(m2l_ops, (1, 2, 0)), root_ops)


def body(offsets, forces, counts, uc2ue, m2m_ops, compress, m2l_ops, root_ops):
    small, block = upward(offsets, forces, counts, uc2ue, m2m_ops, compress)
    local_boxes, local_roots = far_field(small, block, m2l_ops, root_ops)
    return (local_boxes, local_roots)


def solution(mesh):
    placed = (P(None, "morton"), P(None, "morton"), P("morton"), P(), P(), P(), P(), P())
    return jax.shard_map(
        body, mesh=mesh, in_specs=placed, out_specs=(P("morton", None), P()), check_vma=False
    )
```

```python
import functools

import jax
import jax.numpy as jnp
import numpy as np
from jax import lax
from jax.experimental import pallas as pl
from jax.experimental.pallas import tpu as pltpu
from jax.sharding import PartitionSpec as P

SURF_ORDER = 6
NCOEF = 456
RANK = 64
P_CAP = 128
LEAF_DEV = 64
HALF = RANK // 2
PITCH = HALF + 8
FIRST_ROOT = (LEAF_DEV + 9 + 7) // 8 * 8


check_radius = 1.475
MESH = pl.DeviceIdType.MESH


def surface_points():
    tick_values = np.linspace(-1.0, 1.0, SURF_ORDER)
    chosen = []
    for along_x in range(SURF_ORDER):
        for along_y in range(SURF_ORDER):
            for along_z in range(SURF_ORDER):
                if (
                    min(along_x, along_y, along_z) == 0
                    or max(along_x, along_y, along_z) == SURF_ORDER - 1
                ):
                    chosen.append(
                        (tick_values[along_x], tick_values[along_y], tick_values[along_z])
                    )
    return check_radius * np.array(chosen).T


def two_parts(value):
    high = value.astype(jnp.bfloat16).astype(jnp.float32)
    return high, value - high


def product(value, high, low, contracted=0):
    rows = value.shape[0]
    parts = jnp.concatenate(two_parts(value), axis=0).astype(jnp.bfloat16)
    dims = (((1,), (contracted,)), ((), ()))
    both = lax.dot_general(parts, low, dims, preferred_element_type=jnp.float32)
    both += lax.dot_general(parts, high, dims, preferred_element_type=jnp.float32)
    return both[:rows] + both[rows:]


def halves(matrix):
    high, low = two_parts(matrix)
    return high.astype(jnp.bfloat16), low.astype(jnp.bfloat16)


def solver_kernel(peers, counts_ref, offsets_hbm, forces_hbm, targets_hbm, uc2ue_hbm, compress_hbm, m2m_hbm, stored_hbm, root_hbm,
                  packed_ref,
                  offsets_ref, forces_ref, targets_ref, uc2ue_ref, compress_ref, m2m, m2m_high, m2m_low, stored_ref, root_ref, check,
                  small_ref, block_ref, every, nearby, leaf_rows, mid_rows, operator_rows, padded,
                  loads, arrivals, send_all, recv_all, send_near, recv_near):
    f32, bf16 = jnp.float32, jnp.bfloat16
    points = NCOEF // 3
    me = lax.axis_index("morton")
    columns_x, root_count = peers // 4, peers // 8
    column, y_bit, z_bit = me // 4, me // 2 % 2, me % 2
    own, octant = me % 4, me % 8

    wholes = (
        (offsets_hbm, offsets_ref),
        (forces_hbm, forces_ref),
        (targets_hbm, targets_ref),
        (uc2ue_hbm, uc2ue_ref),
        (compress_hbm, compress_ref),
        (stored_hbm, stored_ref),
        (root_hbm, root_ref),
    )

    def load(number):
        return pltpu.make_async_copy(*wholes[number], loads.at[number])

    for number in range(5):
        load(number).start()
    for o in range(8):
        pltpu.make_async_copy(m2m_hbm.at[o], m2m.at[o], arrivals.at[o]).start()
    for number in range(5, 7):
        load(number).start()

    barrier = pltpu.get_barrier_semaphore()

    def greet(k, carry):
        pl.semaphore_signal(barrier, inc=1, device_id=((me + k) % peers,), device_id_type=MESH)
        return carry

    lax.fori_loop(1, peers, greet, 0)

    parts = {-1: (0, 32), 0: (0, 48), 1: (16, 48)}

    def near_copy(number, arriving=False):
        dc, flip_y, flip_z = number // 4 - 1, number // 2 % 2, number % 2
        other = (y_bit + flip_y) % 2 * 2 + (z_bit + flip_z) % 2
        peer = (column + dc + columns_x) % columns_x * 4 + other
        first, last = parts[dc]
        return pltpu.make_async_remote_copy(
            src_ref=block_ref.at[first:last],
            dst_ref=nearby.at[1 - dc, other if arriving else own, first:last],
            send_sem=send_near.at[number], recv_sem=recv_near.at[number],
            device_id=(peer,), device_id_type=MESH)

    def small_copy(k, slot):
        return pltpu.make_async_remote_copy(
            src_ref=small_ref, dst_ref=every.at[pl.ds(slot, 1)], send_sem=send_all.at[k],
            recv_sem=recv_all.at[k], device_id=((me + k) % peers,), device_id_type=MESH)

    for number in range(3):
        load(number).wait()
    check[...] = jnp.zeros_like(check)
    lane = lax.broadcasted_iota(jnp.int32, (8, 128), 1)
    lane_row = lax.broadcasted_iota(jnp.int32, (1, 128), 1)

    def one_leaf(leaf, carry):
        odd = (leaf >> 4 & 1) * 4 + (leaf >> 2 & 1) * 2 + (leaf & 1)
        parent = (leaf >> 5 & 1) * 4 + (leaf >> 3 & 1) * 2 + (leaf >> 1 & 1)
        here = lane == odd * 8 + parent
        slots = pl.ds(pl.multiple_of(leaf * P_CAP, P_CAP), P_CAP)
        live = lane_row < counts_ref[leaf]
        place = [jnp.broadcast_to(offsets_ref[s : s + 1, slots], (8, P_CAP)) for s in range(3)]
        force = [
            jnp.broadcast_to(jnp.where(live, forces_ref[s : s + 1, slots], 0.0), (8, P_CAP))
            for s in range(3)
        ]
        for first in range(0, points, 8):
            apart = [targets_ref[s * points + first : s * points + first + 8] - place[s] for s in range(3)]
            inverse = lax.rsqrt(apart[0] * apart[0] + apart[1] * apart[1] + apart[2] * apart[2])
            projected = apart[0] * force[0] + apart[1] * force[1] + apart[2] * force[2]
            scaled = projected * inverse * inverse
            for s in range(3):
                value = (force[s] + apart[s] * scaled) * inverse
                summed = jnp.sum(value, axis=1, keepdims=True)
                rows = slice(s * points + first, s * points + first + 8)
                check[rows] = jnp.where(here, summed, check[rows])
        return carry

    lax.fori_loop(0, LEAF_DEV, one_leaf, 0, unroll=2)

    potentials = jnp.transpose(check[...])[:LEAF_DEV, :NCOEF]
    load(3).wait()
    load(4).wait()
    leaf_density = product(potentials, *halves(uc2ue_ref[...]))
    mid_density = jnp.zeros((8, NCOEF), f32)
    for o in range(8):
        pltpu.make_async_copy(m2m_hbm.at[o], m2m.at[o], arrivals.at[o]).wait()
        high, low = halves(m2m[o])
        m2m_high[o] = high
        m2m_low[o] = low
        mid_density += product(leaf_density[8 * o : 8 * o + 8], high, low)
    shrink = halves(compress_ref[...])
    rounded = product(jnp.concatenate([leaf_density, mid_density], axis=0), *shrink, contracted=1).astype(bf16)
    row = lax.broadcasted_iota(jnp.int32, (48, 144), 0)
    col = lax.broadcasted_iota(jnp.int32, (48, 144), 1)
    half = jnp.where(col >= 72, 1, 0)
    odd = half * 4 + (row >> 2 & 1) * 2 + (row & 1)
    parent = (row >> 5) * 4 + (row >> 3 & 1) * 2 + (row >> 1 & 1)
    place = (row & 15) + jnp.where((row & 15) < 4, half * 4 + LEAF_DEV, 2 * LEAF_DEV)
    wanted = jnp.where((row >> 4) == 1, place, odd * 8 + parent)
    order = jnp.where(col - 72 * half == wanted, 1.0, 0.0).astype(bf16)
    nothing = jnp.zeros((72, RANK), bf16)
    pairs = jnp.concatenate(
        [jnp.concatenate([rounded, nothing], axis=1), jnp.concatenate([nothing, rounded], axis=1)], axis=0
    )
    block_ref[...] = jnp.dot(order, pairs, preferred_element_type=f32).astype(bf16)

    pl.semaphore_wait(barrier, peers - 1)
    near_numbers = [number for number in range(12) if number != 4]
    for number in near_numbers:
        near_copy(number).start()
    nearby[1, own] = block_ref[...]

    own_density = jnp.zeros((8, NCOEF), f32)
    for o in range(8):
        child = jnp.broadcast_to(mid_density[o : o + 1], (8, NCOEF))
        own_density += product(child, m2m_high[o], m2m_low[o])
    lifted = product(own_density, m2m_high[octant], m2m_low[octant])
    shrunk = product(jnp.concatenate([own_density, lifted], axis=0), *shrink, contracted=1)
    small_ref[...] = jnp.concatenate([shrunk[0:1].astype(bf16).astype(f32), shrunk[8:9]], axis=1)

    def send_small(k, carry):
        small_copy(k, me).start()
        return carry

    lax.fori_loop(1, peers, send_small, 0)
    every[pl.ds(me, 1)] = small_ref[...]

    load(5).wait()
    directions = stored_ref.shape[2]

    def turn(j, carry):
        pairs = jnp.concatenate([stored_ref[j], stored_ref[j + HALF]], axis=0)
        operator_rows[pl.ds(j, directions, stride=PITCH), :] = jnp.transpose(pairs).astype(f32)
        return carry

    lax.fori_loop(0, HALF, turn, 0, unroll=4)

    row = lax.broadcasted_iota(jnp.int32, (224, 256), 0)
    col = lax.broadcasted_iota(jnp.int32, (224, 256), 1)
    step_y = (row >> 5) - 3
    slot = ((row >> 4) & 1) * 4 + (col >> 6)
    step_z = jnp.where(slot < 4, slot - 3 + 3 * (slot >> 1), slot - 5)
    usable = slot < 7

    def chosen(side_bits, target, source, step, bit):
        target = (bit << side_bits) + target
        return (source - target == step) & (jnp.abs((source >> 1) - (target >> 1)) <= 1)

    leaf_select = (
        usable
        & chosen(2, (row >> 2) & 3, (((col >> 5) & 1) << 2) + ((col >> 2) & 3), step_y, y_bit)
        & chosen(2, row & 3, (((col >> 4) & 1) << 2) + (col & 3), step_z, z_bit)
    )
    leaf_select = jnp.where(leaf_select, 1.0, 0.0).astype(bf16)
    mid_base = (
        usable
        & ((row & 15) < 4)
        & ((col & 15) < 4)
        & chosen(1, (row >> 1) & 1, (((col >> 5) & 1) << 1) + ((col >> 1) & 1), step_y, y_bit)
        & chosen(1, row & 1, (((col >> 4) & 1) << 1) + (col & 1), step_z, z_bit)
    )
    mid_select = jnp.where(mid_base, 1.0, 0.0).astype(bf16)
    on_diagonal = (lax.broadcasted_iota(jnp.int32, (256, 256), 0) >> 6) == (
        (lax.broadcasted_iota(jnp.int32, (256, 256), 1) >> 5) & 3
    )

    blank = jnp.zeros((14, 16, 256), bf16)
    leaf_rows[0] = blank
    leaf_rows[9] = blank
    mid_rows[0] = blank
    mid_rows[7] = blank

    blank = jnp.zeros((14, 16, 256), bf16)
    leaf_rows[0] = blank
    leaf_rows[9] = blank
    mid_rows[0] = blank
    mid_rows[7] = blank
    for number in near_numbers:
        near_copy(number, True).wait_recv()

    for c in range(3):
        inside = (column + c >= 1) & (column + c <= columns_x)
        diagonal = jnp.where(on_diagonal & inside, 1.0, 0.0).astype(bf16)
        for first in range(0, 48, 16):
            if (c, first) in ((0, 0), (2, 32)):
                continue
            stack = nearby[c, :, first : first + 16, :].reshape(64, 128)
            for lx in range(2):
                low = stack[:, RANK * lx : RANK * lx + HALF]
                high = stack[:, RANK * lx + HALF : RANK * lx + RANK]
                wide = jnp.concatenate([low] * 4 + [high] * 4, axis=1)
                sources = jnp.concatenate([wide] * 4, axis=0) * diagonal
                if first == 16:
                    got = jnp.dot(mid_select, sources, preferred_element_type=f32)
                    mid_rows[2 * c + lx + 1] = got.astype(bf16).reshape(14, 16, 256)
                else:
                    got = jnp.dot(leaf_select, sources, preferred_element_type=f32)
                    leaf_rows[4 * c + first // 16 + lx - 1] = got.astype(bf16).reshape(14, 16, 256)

    bases = {-3: 0, -2: 49, 2: 218, 3: 267}
    first_direction = 0
    odd_target = (lax.broadcasted_iota(jnp.int32, (192, 128), 0) >> 4) & 1
    total = jnp.zeros((192, 128), f32)
    for u in range(7):
        part = jnp.zeros((192, 128), f32)
        for v in range(7):

            def operand(quads):
                rows = []
                for lanes in (slice(0, 128), slice(128, 256)):
                    for ref, count in ((leaf_rows, 4), (mid_rows, 2)):
                        pieces = [
                            ref[u : u + count, 2 * v + quad, :, lanes].reshape(16 * count, 128)
                            for quad in quads
                        ]
                        rows.append(jnp.concatenate(pieces, axis=1))
                return jnp.concatenate(rows, axis=0)

            def operators(steps):
                rows = [operator_rows[(first_direction + k) * PITCH : (first_direction + k) * PITCH + HALF] for k in steps]
                return jnp.concatenate(rows, axis=0).astype(bf16)

            if 2 <= u <= 4 and 2 <= v <= 4:
                part += jnp.dot(operand((0,)), operators((0, 1, 2, 3)), preferred_element_type=f32)
                first_direction += 4
            else:
                part += jnp.dot(operand((0, 1)), operators((0, 1, 5, 6, 2, 3, 4, 4)), preferred_element_type=f32)
                first_direction += 7
        if u == 0:
            part = jnp.where(odd_target == 1, part, 0.0)
        if u == 6:
            part = jnp.where(odd_target == 0, part, 0.0)
        total += part
    total = total[:96, :RANK] + total[96:, RANK:]
    packed_ref[1:5] = total[64:68]
    packed_ref[5:9] = total[80:84]
    packed_ref[9:73] = total[:64]

    def small_arrived(k, carry):
        small_copy(k, (me - k + peers) % peers).wait_recv()
        return carry

    lax.fori_loop(1, peers, small_arrived, 0)

    own_total = jnp.zeros((1, RANK), f32)
    for u in (-3, -2, 2, 3):
        other = column + u
        good = (other >= 0) & (other < columns_x)
        if u == -3:
            good = good & (column % 2 == 1)
        if u == 3:
            good = good & (column % 2 == 0)
        wrapped = (other + 4 * columns_x) % columns_x
        part = jnp.zeros((1, RANK), f32)
        for sy in range(2):
            for sz in range(2):
                direction = bases[u] + (sy - y_bit + 3) * 7 + (sz - z_bit + 3)
                source = every[pl.ds(wrapped * 4 + sy * 2 + sz, 1)].astype(bf16)
                rows = pl.ds(pl.multiple_of(direction * PITCH, 8), HALF)
                operator = operator_rows[rows].astype(bf16)
                part += jnp.dot(source[:, :HALF], operator[:, :RANK], preferred_element_type=f32)
                part += jnp.dot(source[:, HALF:RANK], operator[:, RANK:], preferred_element_type=f32)
        own_total += jnp.where(good, part, 0.0)
    packed_ref[0:1] = own_total

    load(6).wait()
    padded[...] = jnp.zeros_like(padded)
    for r in range(root_count):
        padded[root_count + r : root_count + r + 1] = jnp.sum(every[8 * r : 8 * r + 8], axis=0, keepdims=True)
    found = jnp.zeros((root_count, RANK), f32)
    for k in range(2 * root_count - 1):
        distance = k - (root_count - 1)
        if abs(distance) >= 2:
            start = root_count + distance
            source = padded[start : start + root_count, :][:, RANK:].astype(bf16)
            found += jnp.dot(source, root_ref[k], preferred_element_type=f32)
    packed_ref[FIRST_ROOT : FIRST_ROOT + root_count] = found

    for number in near_numbers:
        near_copy(number).wait_send()

    def small_sent(k, carry):
        small_copy(k, me).wait_send()
        return carry

    lax.fori_loop(1, peers, small_sent, 0)


def finish_kernel(packed_ref, boxes_ref, roots_ref):
    boxes_ref[...] = jnp.transpose(packed_ref[...])[:, : LEAF_DEV + 9]
    roots_ref[...] = packed_ref[FIRST_ROOT : FIRST_ROOT + roots_ref.shape[0]]


def body(offsets, forces, counts, uc2ue, m2m_ops, compress, m2l_ops, root_ops):
    f32, bf16 = jnp.float32, jnp.bfloat16
    peers = lax.axis_size("morton")
    root_count = peers // 8
    vmem, anywhere = pl.BlockSpec(memory_space=pltpu.VMEM), pl.BlockSpec(memory_space=pl.ANY)
    targets = np.repeat(surface_points().reshape(NCOEF, 1), P_CAP, axis=1)
    stored = jnp.transpose(m2l_ops, (1, 2, 0))
    directions = m2l_ops.shape[0]
    packed = pl.pallas_call(
        functools.partial(solver_kernel, peers),
        out_shape=jax.ShapeDtypeStruct((FIRST_ROOT + (root_count + 7) // 8 * 8, RANK), f32),
        in_specs=[pl.BlockSpec(memory_space=pltpu.SMEM)] + [anywhere] * 8,
        out_specs=vmem,
        scratch_shapes=[
            pltpu.VMEM(offsets.shape, f32),
            pltpu.VMEM(forces.shape, f32),
            pltpu.VMEM(targets.shape, f32),
            pltpu.VMEM(uc2ue.shape, f32),
            pltpu.VMEM((RANK, NCOEF), f32),
            pltpu.VMEM(m2m_ops.shape, f32),
            pltpu.VMEM(m2m_ops.shape, bf16),
            pltpu.VMEM(m2m_ops.shape, bf16),
            pltpu.VMEM(stored.shape, bf16),
            pltpu.VMEM(root_ops.shape, bf16),
            pltpu.VMEM((512, 128), f32),
            pltpu.VMEM((1, 128), f32),
            pltpu.VMEM((48, 128), bf16),
            pltpu.VMEM((peers, 128), f32),
            pltpu.VMEM((3, 4, 48, 128), bf16),
            pltpu.VMEM((10, 14, 16, 256), bf16),
            pltpu.VMEM((8, 14, 16, 256), bf16),
            pltpu.VMEM((directions * PITCH, 2 * RANK), f32),
            pltpu.VMEM((3 * root_count, 128), f32),
            pltpu.SemaphoreType.DMA((7,)),
            pltpu.SemaphoreType.DMA((8,)),
            pltpu.SemaphoreType.DMA((peers,)),
            pltpu.SemaphoreType.DMA((peers,)),
            pltpu.SemaphoreType.DMA((12,)),
            pltpu.SemaphoreType.DMA((12,)),
        ],
        compiler_params=pltpu.CompilerParams(collective_id=0, has_side_effects=True, vmem_limit_bytes=60 << 20),
    )(counts, offsets, forces, jnp.asarray(targets, dtype=f32), uc2ue, compress.T, m2m_ops, stored, root_ops)
    boxes, roots = pl.pallas_call(
        finish_kernel,
        out_shape=(
            jax.ShapeDtypeStruct((RANK, LEAF_DEV + 9), f32),
            jax.ShapeDtypeStruct((root_count, RANK), f32),
        ),
        in_specs=[vmem],
        out_specs=(vmem, vmem),
    )(packed)
    return jnp.transpose(boxes), roots


def solution(mesh):
    placed = (P(None, "morton"), P(None, "morton"), P("morton"), P(), P(), P(), P(), P())
    return jax.shard_map(
        body, mesh=mesh, in_specs=placed, out_specs=(P("morton", None), P()), check_vma=False
    )
```

```python
import functools

import jax
import jax.numpy as jnp
import numpy as np
from jax import lax
from jax.experimental import pallas as pl
from jax.experimental.pallas import tpu as pltpu
from jax.sharding import PartitionSpec as P

SURF_ORDER = 6
NCOEF = 456
RANK = 64
P_CAP = 128
LEAF_DEV = 64
HALF = RANK // 2
PITCH = HALF + 8
FIRST_ROOT = (LEAF_DEV + 9 + 7) // 8 * 8


check_radius = 1.475
LEAF_PITCH = LEAF_DEV + 8
APART = tuple(3 * SURF_ORDER * s for s in range(3))
SQUARE = tuple(first + SURF_ORDER for first in APART)
ALONG = tuple(first + 2 * SURF_ORDER for first in APART)
FORCE = 9 * SURF_ORDER
MESH = pl.DeviceIdType.MESH


def surface_grid():
    order = range(SURF_ORDER)
    ends = (0, SURF_ORDER - 1)
    surface = [(i, j, k) for i in order for j in order for k in order if i in ends or j in ends or k in ends]
    return surface, [float(np.float32(check_radius * tick)) for tick in np.linspace(-1.0, 1.0, SURF_ORDER)]


def two_parts(value):
    high = value.astype(jnp.bfloat16).astype(jnp.float32)
    return high, value - high


def product(value, high, low, contracted=0):
    rows = value.shape[0]
    parts = jnp.concatenate(two_parts(value), axis=0).astype(jnp.bfloat16)
    dims = (((1,), (contracted,)), ((), ()))
    both = lax.dot_general(parts, low, dims, preferred_element_type=jnp.float32)
    both += lax.dot_general(parts, high, dims, preferred_element_type=jnp.float32)
    return both[:rows] + both[rows:]


def halves(matrix):
    high, low = two_parts(matrix)
    return high.astype(jnp.bfloat16), low.astype(jnp.bfloat16)


def solver_kernel(peers, counts_ref, offsets_hbm, forces_hbm, uc2ue_hbm, compress_hbm, m2m_hbm, stored_hbm, root_hbm,
                  packed_ref,
                  offsets_ref, forces_ref, uc2ue_ref, compress_ref, m2m, m2m_high, m2m_low, stored_ref, root_ref, check,
                  slots_by_leaf, table, sums,
                  small_ref, block_ref, every, nearby, leaf_rows, mid_rows, operator_rows, padded,
                  loads, arrivals, send_all, recv_all, send_near, recv_near):
    f32, bf16 = jnp.float32, jnp.bfloat16
    surface, ticks = surface_grid()
    points = len(surface)
    me = lax.axis_index("morton")
    columns_x, root_count = peers // 4, peers // 8
    column, y_bit, z_bit = me // 4, me // 2 % 2, me % 2
    own, octant = me % 4, me % 8

    wholes = (
        (offsets_hbm, offsets_ref),
        (forces_hbm, forces_ref),
        (stored_hbm, stored_ref),
        (uc2ue_hbm, uc2ue_ref),
        (compress_hbm, compress_ref),
        (root_hbm, root_ref),
    )

    def load(number):
        return pltpu.make_async_copy(*wholes[number], loads.at[number])

    for number in range(5):
        load(number).start()
    for o in range(8):
        pltpu.make_async_copy(m2m_hbm.at[o], m2m.at[o], arrivals.at[o]).start()
    load(5).start()

    barrier = pltpu.get_barrier_semaphore()

    def greet(k, carry):
        pl.semaphore_signal(barrier, inc=1, device_id=((me + k) % peers,), device_id_type=MESH)
        return carry

    lax.fori_loop(1, peers, greet, 0)

    parts = {-1: (0, 32), 0: (0, 48), 1: (16, 48)}

    def near_copy(number, arriving=False):
        dc, flip_y, flip_z = number // 4 - 1, number // 2 % 2, number % 2
        other = (y_bit + flip_y) % 2 * 2 + (z_bit + flip_z) % 2
        peer = (column + dc + columns_x) % columns_x * 4 + other
        first, last = parts[dc]
        return pltpu.make_async_remote_copy(
            src_ref=block_ref.at[first:last],
            dst_ref=nearby.at[1 - dc, other if arriving else own, first:last],
            send_sem=send_near.at[number], recv_sem=recv_near.at[number],
            device_id=(peer,), device_id_type=MESH)

    def small_copy(k, slot):
        return pltpu.make_async_remote_copy(
            src_ref=small_ref, dst_ref=every.at[pl.ds(slot, 1)], send_sem=send_all.at[k],
            recv_sem=recv_all.at[k], device_id=((me + k) % peers,), device_id_type=MESH)

    sums[...] = jnp.zeros_like(sums)
    check[NCOEF:] = jnp.zeros((check.shape[0] - NCOEF, 128), f32)
    load(0).wait()
    load(1).wait()
    lane_row = lax.broadcasted_iota(jnp.int32, (1, P_CAP), 1)

    def place(leaf, carry):
        odd = (leaf >> 4 & 1) * 4 + (leaf >> 2 & 1) * 2 + (leaf & 1)
        parent = (leaf >> 5 & 1) * 4 + (leaf >> 3 & 1) * 2 + (leaf >> 1 & 1)
        slots = pl.ds(pl.multiple_of(leaf * P_CAP, P_CAP), P_CAP)
        live = lane_row < counts_ref[leaf]
        slots_by_leaf[pl.ds(odd * 8 + parent, 3, stride=LEAF_PITCH), :] = offsets_ref[:, slots]
        slots_by_leaf[pl.ds(3 * LEAF_PITCH + odd * 8 + parent, 3, stride=LEAF_PITCH), :] = jnp.where(
            live, forces_ref[:, slots], 0.0
        )
        return carry

    lax.fori_loop(0, LEAF_DEV, place, 0, unroll=8)
    for s in range(6):
        leaves = slots_by_leaf[s * LEAF_PITCH : s * LEAF_PITCH + LEAF_DEV]
        leaves = jnp.concatenate([leaves[:, : P_CAP // 2], leaves[:, P_CAP // 2 :]], axis=0)
        table[:, s if s < 3 else FORCE + s - 3] = jnp.transpose(leaves).reshape(8, 8, 128)

    def prepare(block, carry):
        place = [table[block, s] for s in range(3)]
        force = [table[block, FORCE + s] for s in range(3)]
        for s in range(3):
            for i in range(SURF_ORDER):
                apart = ticks[i] - place[s]
                table[block, APART[s] + i] = apart
                table[block, SQUARE[s] + i] = apart * apart
                table[block, ALONG[s] + i] = apart * force[s]
        return carry

    lax.fori_loop(0, 8, prepare, 0)
    load(2).wait()
    directions = stored_ref.shape[2]

    def turn(j):
        pairs = jnp.concatenate([stored_ref[j], stored_ref[j + HALF]], axis=0)
        operator_rows[pl.ds(j, directions, stride=PITCH), :] = jnp.transpose(pairs).astype(f32)

    def two_blocks(step, carry):
        blocks = (2 * step, 2 * step + 1)
        force = [[table[block, FORCE + s] for s in range(3)] for block in blocks]
        column_now = None
        for q, (i, j, k) in enumerate(surface):
            if q % (points // 8) == 0:
                turn(8 * step + q // (points // 8))
            if (i, j) != column_now:
                column_now = (i, j)
                square = [table[block, SQUARE[0] + i] + table[block, SQUARE[1] + j] for block in blocks]
                along = [table[block, ALONG[0] + i] + table[block, ALONG[1] + j] for block in blocks]
            values = [[], [], []]
            for n, block in enumerate(blocks):
                inverse = lax.rsqrt(square[n] + table[block, SQUARE[2] + k])
                projected = along[n] + table[block, ALONG[2] + k]
                scaled = projected * (inverse * inverse)
                for s, tick in enumerate((i, j, k)):
                    values[s].append((force[n][s] + table[block, APART[s] + tick] * scaled) * inverse)
            for s in range(3):
                rows = slice((s * points + q) * 8, (s * points + q) * 8 + 8)
                sums[rows] += values[s][0] + values[s][1]
        return carry

    lax.fori_loop(0, 4, two_blocks, 0)
    for first in range(0, NCOEF, 8):
        rows = [sums[pl.ds(8 * first + r, 8, stride=8), :] for r in range(8)]
        check[first : first + 8] = ((rows[0] + rows[1]) + (rows[2] + rows[3])) + ((rows[4] + rows[5]) + (rows[6] + rows[7]))
    potentials = jnp.transpose(check[...])[:, :NCOEF]
    potentials = potentials[:LEAF_DEV] + potentials[LEAF_DEV:]
    load(3).wait()
    load(4).wait()
    leaf_density = product(potentials, *halves(uc2ue_ref[...]))
    mid_density = jnp.zeros((8, NCOEF), f32)
    for o in range(8):
        pltpu.make_async_copy(m2m_hbm.at[o], m2m.at[o], arrivals.at[o]).wait()
        high, low = halves(m2m[o])
        m2m_high[o] = high
        m2m_low[o] = low
        mid_density += product(leaf_density[8 * o : 8 * o + 8], high, low)
    shrink = halves(compress_ref[...])
    rounded = product(jnp.concatenate([leaf_density, mid_density], axis=0), *shrink, contracted=1).astype(bf16)
    row = lax.broadcasted_iota(jnp.int32, (48, 144), 0)
    col = lax.broadcasted_iota(jnp.int32, (48, 144), 1)
    half = jnp.where(col >= 72, 1, 0)
    odd = half * 4 + (row >> 2 & 1) * 2 + (row & 1)
    parent = (row >> 5) * 4 + (row >> 3 & 1) * 2 + (row >> 1 & 1)
    place = (row & 15) + jnp.where((row & 15) < 4, half * 4 + LEAF_DEV, 2 * LEAF_DEV)
    wanted = jnp.where((row >> 4) == 1, place, odd * 8 + parent)
    order = jnp.where(col - 72 * half == wanted, 1.0, 0.0).astype(bf16)
    nothing = jnp.zeros((72, RANK), bf16)
    pairs = jnp.concatenate(
        [jnp.concatenate([rounded, nothing], axis=1), jnp.concatenate([nothing, rounded], axis=1)], axis=0
    )
    block_ref[...] = jnp.dot(order, pairs, preferred_element_type=f32).astype(bf16)

    pl.semaphore_wait(barrier, peers - 1)
    near_numbers = [number for number in range(12) if number != 4]
    for number in near_numbers:
        near_copy(number).start()
    nearby[1, own] = block_ref[...]

    own_density = jnp.zeros((8, NCOEF), f32)
    for o in range(8):
        child = jnp.broadcast_to(mid_density[o : o + 1], (8, NCOEF))
        own_density += product(child, m2m_high[o], m2m_low[o])
    lifted = product(own_density, m2m_high[octant], m2m_low[octant])
    shrunk = product(jnp.concatenate([own_density, lifted], axis=0), *shrink, contracted=1)
    small_ref[...] = jnp.concatenate([shrunk[0:1].astype(bf16).astype(f32), shrunk[8:9]], axis=1)

    def send_small(k, carry):
        small_copy(k, me).start()
        return carry

    lax.fori_loop(1, peers, send_small, 0)
    every[pl.ds(me, 1)] = small_ref[...]

    row = lax.broadcasted_iota(jnp.int32, (224, 256), 0)
    col = lax.broadcasted_iota(jnp.int32, (224, 256), 1)
    step_y = (row >> 5) - 3
    slot = ((row >> 4) & 1) * 4 + (col >> 6)
    step_z = jnp.where(slot < 4, slot - 3 + 3 * (slot >> 1), slot - 5)
    usable = slot < 7

    def chosen(side_bits, target, source, step, bit):
        target = (bit << side_bits) + target
        return (source - target == step) & (jnp.abs((source >> 1) - (target >> 1)) <= 1)

    leaf_select = (
        usable
        & chosen(2, (row >> 2) & 3, (((col >> 5) & 1) << 2) + ((col >> 2) & 3), step_y, y_bit)
        & chosen(2, row & 3, (((col >> 4) & 1) << 2) + (col & 3), step_z, z_bit)
    )
    leaf_select = jnp.where(leaf_select, 1.0, 0.0).astype(bf16)
    mid_base = (
        usable
        & ((row & 15) < 4)
        & ((col & 15) < 4)
        & chosen(1, (row >> 1) & 1, (((col >> 5) & 1) << 1) + ((col >> 1) & 1), step_y, y_bit)
        & chosen(1, row & 1, (((col >> 4) & 1) << 1) + (col & 1), step_z, z_bit)
    )
    mid_select = jnp.where(mid_base, 1.0, 0.0).astype(bf16)
    on_diagonal = (lax.broadcasted_iota(jnp.int32, (256, 256), 0) >> 6) == (
        (lax.broadcasted_iota(jnp.int32, (256, 256), 1) >> 5) & 3
    )

    blank = jnp.zeros((14, 16, 256), bf16)
    leaf_rows[0] = blank
    leaf_rows[9] = blank
    mid_rows[0] = blank
    mid_rows[7] = blank

    blank = jnp.zeros((14, 16, 256), bf16)
    leaf_rows[0] = blank
    leaf_rows[9] = blank
    mid_rows[0] = blank
    mid_rows[7] = blank
    for number in near_numbers:
        near_copy(number, True).wait_recv()

    for c in range(3):
        inside = (column + c >= 1) & (column + c <= columns_x)
        diagonal = jnp.where(on_diagonal & inside, 1.0, 0.0).astype(bf16)
        for first in range(0, 48, 16):
            if (c, first) in ((0, 0), (2, 32)):
                continue
            stack = nearby[c, :, first : first + 16, :].reshape(64, 128)
            for lx in range(2):
                low = stack[:, RANK * lx : RANK * lx + HALF]
                high = stack[:, RANK * lx + HALF : RANK * lx + RANK]
                wide = jnp.concatenate([low] * 4 + [high] * 4, axis=1)
                sources = jnp.concatenate([wide] * 4, axis=0) * diagonal
                if first == 16:
                    got = jnp.dot(mid_select, sources, preferred_element_type=f32)
                    mid_rows[2 * c + lx + 1] = got.astype(bf16).reshape(14, 16, 256)
                else:
                    got = jnp.dot(leaf_select, sources, preferred_element_type=f32)
                    leaf_rows[4 * c + first // 16 + lx - 1] = got.astype(bf16).reshape(14, 16, 256)

    bases = {-3: 0, -2: 49, 2: 218, 3: 267}
    first_direction = 0
    odd_target = (lax.broadcasted_iota(jnp.int32, (192, 128), 0) >> 4) & 1
    total = jnp.zeros((192, 128), f32)
    for u in range(7):
        part = jnp.zeros((192, 128), f32)
        for v in range(7):

            def operand(quads):
                rows = []
                for lanes in (slice(0, 128), slice(128, 256)):
                    for ref, count in ((leaf_rows, 4), (mid_rows, 2)):
                        pieces = [
                            ref[u : u + count, 2 * v + quad, :, lanes].reshape(16 * count, 128)
                            for quad in quads
                        ]
                        rows.append(jnp.concatenate(pieces, axis=1))
                return jnp.concatenate(rows, axis=0)

            def operators(steps):
                rows = [operator_rows[(first_direction + k) * PITCH : (first_direction + k) * PITCH + HALF] for k in steps]
                return jnp.concatenate(rows, axis=0).astype(bf16)

            if 2 <= u <= 4 and 2 <= v <= 4:
                part += jnp.dot(operand((0,)), operators((0, 1, 2, 3)), preferred_element_type=f32)
                first_direction += 4
            else:
                part += jnp.dot(operand((0, 1)), operators((0, 1, 5, 6, 2, 3, 4, 4)), preferred_element_type=f32)
                first_direction += 7
        if u == 0:
            part = jnp.where(odd_target == 1, part, 0.0)
        if u == 6:
            part = jnp.where(odd_target == 0, part, 0.0)
        total += part
    total = total[:96, :RANK] + total[96:, RANK:]
    packed_ref[1:5] = total[64:68]
    packed_ref[5:9] = total[80:84]
    packed_ref[9:73] = total[:64]

    def small_arrived(k, carry):
        small_copy(k, (me - k + peers) % peers).wait_recv()
        return carry

    lax.fori_loop(1, peers, small_arrived, 0)

    own_total = jnp.zeros((1, RANK), f32)
    for u in (-3, -2, 2, 3):
        other = column + u
        good = (other >= 0) & (other < columns_x)
        if u == -3:
            good = good & (column % 2 == 1)
        if u == 3:
            good = good & (column % 2 == 0)
        wrapped = (other + 4 * columns_x) % columns_x
        part = jnp.zeros((1, RANK), f32)
        for sy in range(2):
            for sz in range(2):
                direction = bases[u] + (sy - y_bit + 3) * 7 + (sz - z_bit + 3)
                source = every[pl.ds(wrapped * 4 + sy * 2 + sz, 1)].astype(bf16)
                rows = pl.ds(pl.multiple_of(direction * PITCH, 8), HALF)
                operator = operator_rows[rows].astype(bf16)
                part += jnp.dot(source[:, :HALF], operator[:, :RANK], preferred_element_type=f32)
                part += jnp.dot(source[:, HALF:RANK], operator[:, RANK:], preferred_element_type=f32)
        own_total += jnp.where(good, part, 0.0)
    packed_ref[0:1] = own_total

    load(5).wait()
    padded[...] = jnp.zeros_like(padded)
    for r in range(root_count):
        padded[root_count + r : root_count + r + 1] = jnp.sum(every[8 * r : 8 * r + 8], axis=0, keepdims=True)
    found = jnp.zeros((root_count, RANK), f32)
    for k in range(2 * root_count - 1):
        distance = k - (root_count - 1)
        if abs(distance) >= 2:
            start = root_count + distance
            source = padded[start : start + root_count, :][:, RANK:].astype(bf16)
            found += jnp.dot(source, root_ref[k], preferred_element_type=f32)
    packed_ref[FIRST_ROOT : FIRST_ROOT + root_count] = found

    for number in near_numbers:
        near_copy(number).wait_send()

    def small_sent(k, carry):
        small_copy(k, me).wait_send()
        return carry

    lax.fori_loop(1, peers, small_sent, 0)


def finish_kernel(packed_ref, boxes_ref, roots_ref):
    boxes_ref[...] = jnp.transpose(packed_ref[...])[:, : LEAF_DEV + 9]
    roots_ref[...] = packed_ref[FIRST_ROOT : FIRST_ROOT + roots_ref.shape[0]]


def body(offsets, forces, counts, uc2ue, m2m_ops, compress, m2l_ops, root_ops):
    f32, bf16 = jnp.float32, jnp.bfloat16
    peers = lax.axis_size("morton")
    root_count = peers // 8
    vmem, anywhere = pl.BlockSpec(memory_space=pltpu.VMEM), pl.BlockSpec(memory_space=pl.ANY)
    stored = jnp.transpose(m2l_ops, (1, 2, 0))
    directions = m2l_ops.shape[0]
    packed = pl.pallas_call(
        functools.partial(solver_kernel, peers),
        out_shape=jax.ShapeDtypeStruct((FIRST_ROOT + (root_count + 7) // 8 * 8, RANK), f32),
        in_specs=[pl.BlockSpec(memory_space=pltpu.SMEM)] + [anywhere] * 7,
        out_specs=vmem,
        scratch_shapes=[
            pltpu.VMEM(offsets.shape, f32),
            pltpu.VMEM(forces.shape, f32),
            pltpu.VMEM(uc2ue.shape, f32),
            pltpu.VMEM((RANK, NCOEF), f32),
            pltpu.VMEM(m2m_ops.shape, f32),
            pltpu.VMEM(m2m_ops.shape, bf16),
            pltpu.VMEM(m2m_ops.shape, bf16),
            pltpu.VMEM(stored.shape, bf16),
            pltpu.VMEM(root_ops.shape, bf16),
            pltpu.VMEM((512, 128), f32),
            pltpu.VMEM((6 * LEAF_PITCH, P_CAP), f32),
            pltpu.VMEM((8, FORCE + 3, 8, 128), f32),
            pltpu.VMEM((8 * NCOEF, 128), f32),
            pltpu.VMEM((1, 128), f32),
            pltpu.VMEM((48, 128), bf16),
            pltpu.VMEM((peers, 128), f32),
            pltpu.VMEM((3, 4, 48, 128), bf16),
            pltpu.VMEM((10, 14, 16, 256), bf16),
            pltpu.VMEM((8, 14, 16, 256), bf16),
            pltpu.VMEM((directions * PITCH, 2 * RANK), f32),
            pltpu.VMEM((3 * root_count, 128), f32),
            pltpu.SemaphoreType.DMA((6,)),
            pltpu.SemaphoreType.DMA((8,)),
            pltpu.SemaphoreType.DMA((peers,)),
            pltpu.SemaphoreType.DMA((peers,)),
            pltpu.SemaphoreType.DMA((12,)),
            pltpu.SemaphoreType.DMA((12,)),
        ],
        compiler_params=pltpu.CompilerParams(collective_id=0, has_side_effects=True, vmem_limit_bytes=60 << 20),
    )(counts, offsets, forces, uc2ue, compress.T, m2m_ops, stored, root_ops)
    boxes, roots = pl.pallas_call(
        finish_kernel,
        out_shape=(
            jax.ShapeDtypeStruct((RANK, LEAF_DEV + 9), f32),
            jax.ShapeDtypeStruct((root_count, RANK), f32),
        ),
        in_specs=[vmem],
        out_specs=(vmem, vmem),
        compiler_params=pltpu.CompilerParams(vmem_limit_bytes=1 << 20),
    )(packed)
    return jnp.transpose(boxes), roots


def solution(mesh):
    placed = (P(None, "morton"), P(None, "morton"), P("morton"), P(), P(), P(), P(), P())
    return jax.shard_map(
        body, mesh=mesh, in_specs=placed, out_specs=(P("morton", None), P()), check_vma=False
    )
```

```python
import functools

import jax
import jax.numpy as jnp
import numpy as np
from jax import lax
from jax.experimental import pallas as pl
from jax.experimental.pallas import tpu as pltpu
from jax.sharding import PartitionSpec as P

SURF_ORDER = 6
NCOEF = 456
RANK = 64
P_CAP = 128
LEAF_DEV = 64
HALF = RANK // 2
PITCH = HALF + 8
FIRST_ROOT = (LEAF_DEV + 9 + 7) // 8 * 8


check_radius = 1.475
LEAF_PITCH = LEAF_DEV + 8
APART = tuple(3 * SURF_ORDER * s for s in range(3))
SQUARE = tuple(first + SURF_ORDER for first in APART)
ALONG = tuple(first + 2 * SURF_ORDER for first in APART)
FORCE = 9 * SURF_ORDER
MESH = pl.DeviceIdType.MESH


def surface_grid():
    order = range(SURF_ORDER)
    ends = (0, SURF_ORDER - 1)
    surface = [(i, j, k) for i in order for j in order for k in order if i in ends or j in ends or k in ends]
    return surface, [float(np.float32(check_radius * tick)) for tick in np.linspace(-1.0, 1.0, SURF_ORDER)]


def two_parts(value):
    high = value.astype(jnp.bfloat16).astype(jnp.float32)
    return high, value - high


def product(value, high, low):
    rows = value.shape[0]
    parts = two_bf16(value)
    both = jnp.dot(parts, low, preferred_element_type=jnp.float32)
    both += jnp.dot(parts, high, preferred_element_type=jnp.float32)
    return both[:rows] + both[rows:]


def two_bf16(value):
    return jnp.concatenate(two_parts(value), axis=0).astype(jnp.bfloat16)


def shrunk(parts, shrink):
    dims = (((1,), (1,)), ((), ()))
    both = lax.dot_general(parts, shrink, dims, preferred_element_type=jnp.float32)
    rows, rank = parts.shape[0] // 2, shrink.shape[0] // 2
    both = both[:rows] + both[rows:]
    return both[:, :rank] + both[:, rank:]


def halves(matrix):
    high, low = two_parts(matrix)
    return high.astype(jnp.bfloat16), low.astype(jnp.bfloat16)


def solver_kernel(peers, counts_ref, offsets_hbm, forces_hbm, uc2ue_hbm, compress_hbm, m2m_hbm, stored_hbm, root_hbm,
                  packed_ref,
                  offsets_ref, forces_ref, uc2ue_ref, compress_ref, m2m, m2m_high, m2m_low, stored_ref, root_ref, check,
                  slots_by_leaf, table, sums,
                  small_ref, block_ref, every, nearby, leaf_rows, mid_rows, operator_rows, padded,
                  loads, arrivals, send_all, recv_all, send_near, recv_near):
    f32, bf16 = jnp.float32, jnp.bfloat16
    surface, ticks = surface_grid()
    points = len(surface)
    me = lax.axis_index("morton")
    columns_x, root_count = peers // 4, peers // 8
    column, y_bit, z_bit = me // 4, me // 2 % 2, me % 2
    own, octant = me % 4, me % 8

    wholes = (
        (offsets_hbm, offsets_ref),
        (forces_hbm, forces_ref),
        (uc2ue_hbm, uc2ue_ref),
        (compress_hbm, compress_ref),
        (stored_hbm, stored_ref),
        (root_hbm, root_ref),
    )

    def load(number):
        return pltpu.make_async_copy(*wholes[number], loads.at[number])

    for number in range(4):
        load(number).start()
    for o in range(8):
        pltpu.make_async_copy(m2m_hbm.at[o], m2m.at[o], arrivals.at[o]).start()
    load(4).start()
    load(5).start()

    def around(k):
        return jnp.where(me + k >= peers, me + k - peers, me + k)

    barrier = pltpu.get_barrier_semaphore()

    def greet(k, carry):
        pl.semaphore_signal(barrier, inc=1, device_id=(around(k),), device_id_type=MESH)
        return carry

    lax.fori_loop(1, peers, greet, 0, unroll=4)

    parts = {-1: (0, 32), 0: (0, 48), 1: (16, 48)}

    def near_copy(number):
        dc, flip_y, flip_z = number // 4 - 1, number // 2 % 2, number % 2
        other = (y_bit + flip_y) % 2 * 2 + (z_bit + flip_z) % 2
        peer = (column + dc + columns_x) % columns_x * 4 + other
        first, last = parts[dc]
        return pltpu.make_async_remote_copy(
            src_ref=block_ref.at[first:last],
            dst_ref=nearby.at[1 - dc, own, first:last],
            send_sem=send_near.at[1 - dc], recv_sem=recv_near.at[1 - dc],
            device_id=(peer,), device_id_type=MESH)

    def near_whole(c):
        count, (first, last) = (3 if c == 1 else 4), parts[1 - c]
        space = nearby.at[c, 0:count, first:last]
        return pltpu.make_async_remote_copy(
            src_ref=space, dst_ref=space, send_sem=send_near.at[c], recv_sem=recv_near.at[c],
            device_id=(me,), device_id_type=MESH)

    def small_copy(k):
        return pltpu.make_async_remote_copy(
            src_ref=small_ref, dst_ref=every.at[pl.ds(me, 1)], send_sem=send_all, recv_sem=recv_all,
            device_id=(around(k),), device_id_type=MESH)

    def small_whole():
        space = every.at[0 : peers - 1]
        return pltpu.make_async_remote_copy(
            src_ref=space, dst_ref=space, send_sem=send_all, recv_sem=recv_all,
            device_id=(me,), device_id_type=MESH)

    sums[...] = jnp.zeros_like(sums)
    check[NCOEF:] = jnp.zeros((check.shape[0] - NCOEF, 128), f32)
    load(0).wait()
    load(1).wait()
    lane_row = lax.broadcasted_iota(jnp.int32, (1, P_CAP), 1)

    def place(leaf, carry):
        odd = (leaf >> 4 & 1) * 4 + (leaf >> 2 & 1) * 2 + (leaf & 1)
        parent = (leaf >> 5 & 1) * 4 + (leaf >> 3 & 1) * 2 + (leaf >> 1 & 1)
        slots = pl.ds(pl.multiple_of(leaf * P_CAP, P_CAP), P_CAP)
        live = lane_row < counts_ref[leaf]
        slots_by_leaf[pl.ds(odd * 8 + parent, 3, stride=LEAF_PITCH), :] = offsets_ref[:, slots]
        slots_by_leaf[pl.ds(3 * LEAF_PITCH + odd * 8 + parent, 3, stride=LEAF_PITCH), :] = jnp.where(
            live, forces_ref[:, slots], 0.0
        )
        return carry

    lax.fori_loop(0, LEAF_DEV, place, 0, unroll=8)
    for s in range(6):
        leaves = slots_by_leaf[s * LEAF_PITCH : s * LEAF_PITCH + LEAF_DEV]
        leaves = jnp.concatenate([leaves[:, : P_CAP // 2], leaves[:, P_CAP // 2 :]], axis=0)
        table[:, s if s < 3 else FORCE + s - 3] = jnp.transpose(leaves).reshape(8, 8, 128)

    def prepare(block, carry):
        place = [table[block, s] for s in range(3)]
        force = [table[block, FORCE + s] for s in range(3)]
        for s in range(3):
            for i in range(SURF_ORDER):
                apart = ticks[i] - place[s]
                table[block, APART[s] + i] = apart
                table[block, SQUARE[s] + i] = apart * apart
                table[block, ALONG[s] + i] = apart * force[s]
        return carry

    lax.fori_loop(0, 8, prepare, 0)
    def two_blocks(step, carry):
        blocks = (2 * step, 2 * step + 1)
        force = [[table[block, FORCE + s] for s in range(3)] for block in blocks]
        column_now = None
        for q, (i, j, k) in enumerate(surface):
            if (i, j) != column_now:
                column_now = (i, j)
                square = [table[block, SQUARE[0] + i] + table[block, SQUARE[1] + j] for block in blocks]
                along = [table[block, ALONG[0] + i] + table[block, ALONG[1] + j] for block in blocks]
            values = [[], [], []]
            for n, block in enumerate(blocks):
                inverse = lax.rsqrt(square[n] + table[block, SQUARE[2] + k])
                projected = along[n] + table[block, ALONG[2] + k]
                scaled = projected * (inverse * inverse)
                for s, tick in enumerate((i, j, k)):
                    values[s].append((force[n][s] + table[block, APART[s] + tick] * scaled) * inverse)
            for s in range(3):
                rows = slice((s * points + q) * 8, (s * points + q) * 8 + 8)
                sums[rows] += values[s][0] + values[s][1]
        return carry

    lax.fori_loop(0, 4, two_blocks, 0)
    for first in range(0, NCOEF, 8):
        rows = [sums[pl.ds(8 * first + r, 8, stride=8), :] for r in range(8)]
        check[first : first + 8] = ((rows[0] + rows[1]) + (rows[2] + rows[3])) + ((rows[4] + rows[5]) + (rows[6] + rows[7]))
    potentials = jnp.transpose(check[...])[:, :NCOEF]
    potentials = potentials[:LEAF_DEV] + potentials[LEAF_DEV:]
    load(2).wait()
    load(3).wait()
    leaf_density = product(potentials, *halves(uc2ue_ref[...]))
    mid_density = jnp.zeros((8, NCOEF), f32)
    for o in range(8):
        pltpu.make_async_copy(m2m_hbm.at[o], m2m.at[o], arrivals.at[o]).wait()
        high, low = halves(m2m[o])
        m2m_high[o] = high
        m2m_low[o] = low
        mid_density += product(leaf_density[8 * o : 8 * o + 8], high, low)
    shrink = jnp.concatenate(halves(compress_ref[...]), axis=0)
    rounded = shrunk(two_bf16(jnp.concatenate([leaf_density, mid_density], axis=0)), shrink).astype(bf16)
    row = lax.broadcasted_iota(jnp.int32, (48, 144), 0)
    col = lax.broadcasted_iota(jnp.int32, (48, 144), 1)
    half = jnp.where(col >= 72, 1, 0)
    odd = half * 4 + (row >> 2 & 1) * 2 + (row & 1)
    parent = (row >> 5) * 4 + (row >> 3 & 1) * 2 + (row >> 1 & 1)
    place = (row & 15) + jnp.where((row & 15) < 4, half * 4 + LEAF_DEV, 2 * LEAF_DEV)
    wanted = jnp.where((row >> 4) == 1, place, odd * 8 + parent)
    order = jnp.where(col - 72 * half == wanted, 1.0, 0.0).astype(bf16)
    nothing = jnp.zeros((72, RANK), bf16)
    pairs = jnp.concatenate(
        [jnp.concatenate([rounded, nothing], axis=1), jnp.concatenate([nothing, rounded], axis=1)], axis=0
    )
    block_ref[...] = jnp.dot(order, pairs, preferred_element_type=f32).astype(bf16)

    pl.semaphore_wait(barrier, peers - 1)
    near_numbers = [number for number in range(12) if number != 4]
    for number in near_numbers:
        near_copy(number).start()
    nearby[1, own] = block_ref[...]

    load(4).wait()
    directions = stored_ref.shape[2]

    def turn(j, carry):
        pairs = jnp.concatenate([stored_ref[j], stored_ref[j + HALF]], axis=0)
        operator_rows[pl.ds(j, directions, stride=PITCH), :] = jnp.transpose(pairs).astype(f32)
        return carry

    for j in range(HALF):
        turn(j, 0)
    lift = shrunk(jnp.concatenate([m2m_high[octant], m2m_low[octant]], axis=0), shrink)
    own_density = jnp.zeros((8, NCOEF), f32)
    for o in range(8):
        child = jnp.broadcast_to(mid_density[o : o + 1], (8, NCOEF))
        own_density += product(child, m2m_high[o], m2m_low[o])
    lifted = product(own_density, *halves(lift))
    own_multipole = shrunk(two_bf16(own_density), shrink).astype(bf16).astype(f32)
    small_ref[...] = jnp.concatenate([own_multipole[:1], lifted[:1]], axis=1)

    def send_small(k, carry):
        small_copy(k).start()
        return carry

    lax.fori_loop(1, peers, send_small, 0, unroll=4)
    every[pl.ds(me, 1)] = small_ref[...]

    row = lax.broadcasted_iota(jnp.int32, (224, 256), 0)
    col = lax.broadcasted_iota(jnp.int32, (224, 256), 1)
    step_y = (row >> 5) - 3
    slot = ((row >> 4) & 1) * 4 + (col >> 6)
    step_z = jnp.where(slot < 4, slot - 3 + 3 * (slot >> 1), slot - 5)
    usable = slot < 7

    def chosen(side_bits, target, source, step, bit):
        target = (bit << side_bits) + target
        return (source - target == step) & (jnp.abs((source >> 1) - (target >> 1)) <= 1)

    leaf_select = (
        usable
        & chosen(2, (row >> 2) & 3, (((col >> 5) & 1) << 2) + ((col >> 2) & 3), step_y, y_bit)
        & chosen(2, row & 3, (((col >> 4) & 1) << 2) + (col & 3), step_z, z_bit)
    )
    leaf_select = jnp.where(leaf_select, 1.0, 0.0).astype(bf16)
    mid_base = (
        usable
        & ((row & 15) < 4)
        & ((col & 15) < 4)
        & chosen(1, (row >> 1) & 1, (((col >> 5) & 1) << 1) + ((col >> 1) & 1), step_y, y_bit)
        & chosen(1, row & 1, (((col >> 4) & 1) << 1) + (col & 1), step_z, z_bit)
    )
    mid_select = jnp.where(mid_base, 1.0, 0.0).astype(bf16)
    on_diagonal = (lax.broadcasted_iota(jnp.int32, (256, 256), 0) >> 6) == (
        (lax.broadcasted_iota(jnp.int32, (256, 256), 1) >> 5) & 3
    )

    blank = jnp.zeros((14, 16, 256), bf16)
    leaf_rows[0] = blank
    leaf_rows[9] = blank
    mid_rows[0] = blank
    mid_rows[7] = blank

    blank = jnp.zeros((14, 16, 256), bf16)
    leaf_rows[0] = blank
    leaf_rows[9] = blank
    mid_rows[0] = blank
    mid_rows[7] = blank
    for c in range(3):
        near_whole(c).wait_recv()

    for c in range(3):
        inside = (column + c >= 1) & (column + c <= columns_x)
        diagonal = jnp.where(on_diagonal & inside, 1.0, 0.0).astype(bf16)
        for first in range(0, 48, 16):
            if (c, first) in ((0, 0), (2, 32)):
                continue
            stack = nearby[c, :, first : first + 16, :].reshape(64, 128)
            for lx in range(2):
                low = stack[:, RANK * lx : RANK * lx + HALF]
                high = stack[:, RANK * lx + HALF : RANK * lx + RANK]
                wide = jnp.concatenate([low] * 4 + [high] * 4, axis=1)
                sources = jnp.concatenate([wide] * 4, axis=0) * diagonal
                if first == 16:
                    got = jnp.dot(mid_select, sources, preferred_element_type=f32)
                    mid_rows[2 * c + lx + 1] = got.astype(bf16).reshape(14, 16, 256)
                else:
                    got = jnp.dot(leaf_select, sources, preferred_element_type=f32)
                    leaf_rows[4 * c + first // 16 + lx - 1] = got.astype(bf16).reshape(14, 16, 256)

    bases = {-3: 0, -2: 49, 2: 218, 3: 267}
    first_direction = 0
    odd_target = (lax.broadcasted_iota(jnp.int32, (192, 128), 0) >> 4) & 1
    total = jnp.zeros((192, 128), f32)
    for u in range(7):
        part = jnp.zeros((192, 128), f32)
        for v in range(7):

            def operand(quads):
                rows = []
                for lanes in (slice(0, 128), slice(128, 256)):
                    for ref, count in ((leaf_rows, 4), (mid_rows, 2)):
                        pieces = [
                            ref[u : u + count, 2 * v + quad, :, lanes].reshape(16 * count, 128)
                            for quad in quads
                        ]
                        rows.append(jnp.concatenate(pieces, axis=1))
                return jnp.concatenate(rows, axis=0)

            def operators(steps):
                rows = [operator_rows[(first_direction + k) * PITCH : (first_direction + k) * PITCH + HALF] for k in steps]
                return jnp.concatenate(rows, axis=0).astype(bf16)

            if 2 <= u <= 4 and 2 <= v <= 4:
                part += jnp.dot(operand((0,)), operators((0, 1, 2, 3)), preferred_element_type=f32)
                first_direction += 4
            else:
                part += jnp.dot(operand((0, 1)), operators((0, 1, 5, 6, 2, 3, 4, 4)), preferred_element_type=f32)
                first_direction += 7
        if u == 0:
            part = jnp.where(odd_target == 1, part, 0.0)
        if u == 6:
            part = jnp.where(odd_target == 0, part, 0.0)
        total += part
    total = total[:96, :RANK] + total[96:, RANK:]
    packed_ref[1:5] = total[64:68]
    packed_ref[5:9] = total[80:84]
    packed_ref[9:73] = total[:64]

    small_whole().wait_recv()
    own_total = jnp.zeros((1, RANK), f32)
    for u in (-3, -2, 2, 3):
        other = column + u
        good = (other >= 0) & (other < columns_x)
        if u == -3:
            good = good & (column % 2 == 1)
        if u == 3:
            good = good & (column % 2 == 0)
        wrapped = (other + 4 * columns_x) % columns_x
        part = jnp.zeros((1, RANK), f32)
        for sy in range(2):
            for sz in range(2):
                direction = bases[u] + (sy - y_bit + 3) * 7 + (sz - z_bit + 3)
                source = every[pl.ds(wrapped * 4 + sy * 2 + sz, 1)].astype(bf16)
                rows = pl.ds(pl.multiple_of(direction * PITCH, 8), HALF)
                operator = operator_rows[rows].astype(bf16)
                part += jnp.dot(source[:, :HALF], operator[:, :RANK], preferred_element_type=f32)
                part += jnp.dot(source[:, HALF:RANK], operator[:, RANK:], preferred_element_type=f32)
        own_total += jnp.where(good, part, 0.0)
    packed_ref[0:1] = own_total

    load(5).wait()
    padded[...] = jnp.zeros_like(padded)
    for r in range(root_count):
        padded[root_count + r : root_count + r + 1] = jnp.sum(every[8 * r : 8 * r + 8], axis=0, keepdims=True)
    found = jnp.zeros((root_count, RANK), f32)
    for k in range(2 * root_count - 1):
        distance = k - (root_count - 1)
        if abs(distance) >= 2:
            start = root_count + distance
            source = padded[start : start + root_count, :][:, RANK:].astype(bf16)
            found += jnp.dot(source, root_ref[k], preferred_element_type=f32)
    packed_ref[FIRST_ROOT : FIRST_ROOT + root_count] = found

    for c in range(3):
        near_whole(c).wait_send()
    small_whole().wait_send()


def finish_kernel(packed_ref, boxes_ref, roots_ref):
    boxes_ref[...] = jnp.transpose(packed_ref[...])[:, : LEAF_DEV + 9]
    roots_ref[...] = packed_ref[FIRST_ROOT : FIRST_ROOT + roots_ref.shape[0]]


def body(offsets, forces, counts, uc2ue, m2m_ops, compress, m2l_ops, root_ops):
    f32, bf16 = jnp.float32, jnp.bfloat16
    peers = lax.axis_size("morton")
    root_count = peers // 8
    vmem, anywhere = pl.BlockSpec(memory_space=pltpu.VMEM), pl.BlockSpec(memory_space=pl.ANY)
    stored = jnp.transpose(m2l_ops, (1, 2, 0))
    directions = m2l_ops.shape[0]
    packed = pl.pallas_call(
        functools.partial(solver_kernel, peers),
        out_shape=pltpu.VMEM((FIRST_ROOT + (root_count + 7) // 8 * 8, RANK), f32),
        in_specs=[pl.BlockSpec(memory_space=pltpu.SMEM)] + [anywhere] * 7,
        out_specs=vmem,
        scratch_shapes=[
            pltpu.VMEM(offsets.shape, f32),
            pltpu.VMEM(forces.shape, f32),
            pltpu.VMEM(uc2ue.shape, f32),
            pltpu.VMEM((RANK, NCOEF), f32),
            pltpu.VMEM(m2m_ops.shape, f32),
            pltpu.VMEM(m2m_ops.shape, bf16),
            pltpu.VMEM(m2m_ops.shape, bf16),
            pltpu.VMEM(stored.shape, bf16),
            pltpu.VMEM(root_ops.shape, bf16),
            pltpu.VMEM((512, 128), f32),
            pltpu.VMEM((6 * LEAF_PITCH, P_CAP), f32),
            pltpu.VMEM((8, FORCE + 3, 8, 128), f32),
            pltpu.VMEM((8 * NCOEF, 128), f32),
            pltpu.VMEM((1, 128), f32),
            pltpu.VMEM((48, 128), bf16),
            pltpu.VMEM((peers, 128), f32),
            pltpu.VMEM((3, 4, 48, 128), bf16),
            pltpu.VMEM((10, 14, 16, 256), bf16),
            pltpu.VMEM((8, 14, 16, 256), bf16),
            pltpu.VMEM((directions * PITCH, 2 * RANK), f32),
            pltpu.VMEM((3 * root_count, 128), f32),
            pltpu.SemaphoreType.DMA((6,)),
            pltpu.SemaphoreType.DMA((8,)),
            pltpu.SemaphoreType.DMA,
            pltpu.SemaphoreType.DMA,
            pltpu.SemaphoreType.DMA((3,)),
            pltpu.SemaphoreType.DMA((3,)),
        ],
        compiler_params=pltpu.CompilerParams(collective_id=0, has_side_effects=True, vmem_limit_bytes=60 << 20),
    )(counts, offsets, forces, uc2ue, compress.T, m2m_ops, stored, root_ops)
    boxes, roots = pl.pallas_call(
        finish_kernel,
        out_shape=(
            jax.ShapeDtypeStruct((RANK, LEAF_DEV + 9), f32),
            jax.ShapeDtypeStruct((root_count, RANK), f32),
        ),
        in_specs=[vmem],
        out_specs=(vmem, vmem),
        compiler_params=pltpu.CompilerParams(vmem_limit_bytes=1 << 20),
    )(packed)
    return jnp.transpose(boxes), roots


def solution(mesh):
    placed = (P(None, "morton"), P(None, "morton"), P("morton"), P(), P(), P(), P(), P())
    return jax.shard_map(
        body, mesh=mesh, in_specs=placed, out_specs=(P("morton", None), P()), check_vma=False
    )
```

```python
import functools

import jax
import jax.numpy as jnp
import numpy as np
from jax import lax
from jax.experimental import pallas as pl
from jax.experimental.pallas import tpu as pltpu
from jax.sharding import PartitionSpec as P

SURF_ORDER = 6
NCOEF = 456
RANK = 64
P_CAP = 128
LEAF_DEV = 64
HALF = RANK // 2
PITCH = HALF + 8
FIRST_ROOT = (LEAF_DEV + 9 + 7) // 8 * 8


check_radius = 1.475
LEAF_PITCH = LEAF_DEV + 8
APART = tuple(3 * SURF_ORDER * s for s in range(3))
SQUARE = tuple(first + SURF_ORDER for first in APART)
ALONG = tuple(first + 2 * SURF_ORDER for first in APART)
FORCE = 9 * SURF_ORDER
MESH = pl.DeviceIdType.MESH


def surface_grid():
    order = range(SURF_ORDER)
    ends = (0, SURF_ORDER - 1)
    surface = [(i, j, k) for i in order for j in order for k in order if i in ends or j in ends or k in ends]
    return surface, [float(np.float32(check_radius * tick)) for tick in np.linspace(-1.0, 1.0, SURF_ORDER)]


def two_parts(value):
    high = value.astype(jnp.bfloat16).astype(jnp.float32)
    return high, value - high


def product(value, high, low):
    rows = value.shape[0]
    parts = two_bf16(value)
    both = jnp.dot(parts, low, preferred_element_type=jnp.float32)
    both += jnp.dot(parts, high, preferred_element_type=jnp.float32)
    return both[:rows] + both[rows:]


def two_bf16(value):
    return jnp.concatenate(two_parts(value), axis=0).astype(jnp.bfloat16)


def shrunk(parts, shrink):
    dims = (((1,), (1,)), ((), ()))
    both = lax.dot_general(parts, shrink, dims, preferred_element_type=jnp.float32)
    rows, rank = parts.shape[0] // 2, shrink.shape[0] // 2
    both = both[:rows] + both[rows:]
    return both[:, :rank] + both[:, rank:]


def halves(matrix):
    high, low = two_parts(matrix)
    return high.astype(jnp.bfloat16), low.astype(jnp.bfloat16)


def solver_kernel(peers, counts_ref, offsets_hbm, forces_hbm, uc2ue_hbm, compress_hbm, m2m_hbm, stored_hbm, root_hbm,
                  packed_ref,
                  offsets_ref, forces_ref, uc2ue_ref, compress_ref, uc2ue_high, uc2ue_low, shrink_parts, m2m, m2m_high, m2m_low, stored_ref, root_ref, check,
                  slots_by_leaf, table, sums,
                  small_ref, block_ref, every, nearby, leaf_rows, mid_rows, operator_rows, padded,
                  loads, arrivals, send_all, recv_all, send_near, recv_near):
    f32, bf16 = jnp.float32, jnp.bfloat16
    surface, ticks = surface_grid()
    points = len(surface)
    me = lax.axis_index("morton")
    columns_x, root_count = peers // 4, peers // 8
    column, y_bit, z_bit = me // 4, me // 2 % 2, me % 2
    own, octant = me % 4, me % 8

    wholes = (
        (offsets_hbm, offsets_ref),
        (forces_hbm, forces_ref),
        (uc2ue_hbm, uc2ue_ref),
        (compress_hbm, compress_ref),
        (stored_hbm, stored_ref),
        (root_hbm, root_ref),
    )

    def load(number):
        return pltpu.make_async_copy(*wholes[number], loads.at[number])

    for number in range(4):
        load(number).start()
    for o in range(8):
        pltpu.make_async_copy(m2m_hbm.at[o], m2m.at[o], arrivals.at[o]).start()
    load(4).start()
    load(5).start()

    def around(k):
        return jnp.where(me + k >= peers, me + k - peers, me + k)

    barrier = pltpu.get_barrier_semaphore()

    def greet(k, carry):
        pl.semaphore_signal(barrier, inc=1, device_id=(around(k),), device_id_type=MESH)
        return carry

    lax.fori_loop(1, peers, greet, 0, unroll=peers - 1 if peers <= 64 else 5)

    parts = {-1: (0, 16), 0: (0, 32), 1: (16, 32)}
    near_numbers = [number for number in range(12) if number != 4]

    def near_copy(number, kind):
        dc, flip_y, flip_z = number // 4 - 1, number // 2 % 2, number % 2
        other = (y_bit + flip_y) % 2 * 2 + (z_bit + flip_z) % 2
        peer = (column + dc + columns_x) % columns_x * 4 + other
        first, last = (32, 48) if kind else parts[dc]
        return pltpu.make_async_remote_copy(
            src_ref=block_ref.at[first:last],
            dst_ref=nearby.at[1 - dc, own, first:last],
            send_sem=send_near.at[kind, 1 - dc], recv_sem=recv_near.at[kind, 1 - dc],
            device_id=(peer,), device_id_type=MESH)

    def near_whole(c, kind):
        count, (first, last) = (3 if c == 1 else 4), ((32, 48) if kind else parts[1 - c])
        space = nearby.at[c, 0:count, first:last]
        return pltpu.make_async_remote_copy(
            src_ref=space, dst_ref=space, send_sem=send_near.at[kind, c], recv_sem=recv_near.at[kind, c],
            device_id=(me,), device_id_type=MESH)

    def small_copy(k):
        return pltpu.make_async_remote_copy(
            src_ref=small_ref, dst_ref=every.at[pl.ds(me, 1)], send_sem=send_all, recv_sem=recv_all,
            device_id=(around(k),), device_id_type=MESH)

    def small_whole():
        space = every.at[0 : peers - 1]
        return pltpu.make_async_remote_copy(
            src_ref=space, dst_ref=space, send_sem=send_all, recv_sem=recv_all,
            device_id=(me,), device_id_type=MESH)

    sums[...] = jnp.zeros_like(sums)
    check[NCOEF:] = jnp.zeros((check.shape[0] - NCOEF, 128), f32)
    load(0).wait()
    load(1).wait()
    lane_row = lax.broadcasted_iota(jnp.int32, (1, P_CAP), 1)

    def place(leaf, carry):
        odd = (leaf >> 4 & 1) * 4 + (leaf >> 2 & 1) * 2 + (leaf & 1)
        parent = (leaf >> 5 & 1) * 4 + (leaf >> 3 & 1) * 2 + (leaf >> 1 & 1)
        slots = pl.ds(pl.multiple_of(leaf * P_CAP, P_CAP), P_CAP)
        live = lane_row < counts_ref[leaf]
        slots_by_leaf[pl.ds(odd * 8 + parent, 3, stride=LEAF_PITCH), :] = offsets_ref[:, slots]
        slots_by_leaf[pl.ds(3 * LEAF_PITCH + odd * 8 + parent, 3, stride=LEAF_PITCH), :] = jnp.where(
            live, forces_ref[:, slots], 0.0
        )
        return carry

    lax.fori_loop(0, LEAF_DEV, place, 0, unroll=16)
    for s in range(6):
        leaves = slots_by_leaf[s * LEAF_PITCH : s * LEAF_PITCH + LEAF_DEV]
        leaves = jnp.concatenate([leaves[:, : P_CAP // 2], leaves[:, P_CAP // 2 :]], axis=0)
        table[:, FORCE + 3 + s if s < 3 else FORCE + s - 3] = jnp.transpose(leaves).reshape(8, 8, 128)

    for block in range(8):
        for s in range(3):
            place, force = table[block, FORCE + 3 + s], table[block, FORCE + s]
            for i in range(SURF_ORDER):
                apart = ticks[i] - place
                table[block, APART[s] + i] = apart
                table[block, SQUARE[s] + i] = apart * apart
                table[block, ALONG[s] + i] = apart * force

    load(2).wait()
    load(3).wait()
    uc2ue_high[...], uc2ue_low[...] = halves(uc2ue_ref[...])
    shrink_parts[...] = jnp.concatenate(halves(compress_ref[...]), axis=0)

    def two_blocks(step, carry):
        blocks = (2 * step, 2 * step + 1)
        for o in blocks:
            pltpu.make_async_copy(m2m_hbm.at[o], m2m.at[o], arrivals.at[o]).wait()
        force = [[table[block, FORCE + s] for s in range(3)] for block in blocks]
        column_now = None
        for q, (i, j, k) in enumerate(surface):
            if (i, j) != column_now:
                column_now = (i, j)
                square = [table[block, SQUARE[0] + i] + table[block, SQUARE[1] + j] for block in blocks]
                along = [table[block, ALONG[0] + i] + table[block, ALONG[1] + j] for block in blocks]
            values = [[], [], []]
            for n, block in enumerate(blocks):
                inverse = lax.rsqrt(square[n] + table[block, SQUARE[2] + k])
                projected = along[n] + table[block, ALONG[2] + k]
                scaled = projected * (inverse * inverse)
                for s, tick in enumerate((i, j, k)):
                    values[s].append((force[n][s] + table[block, APART[s] + tick] * scaled) * inverse)
            for s in range(3):
                rows = slice((s * points + q) * 8, (s * points + q) * 8 + 8)
                sums[rows] += values[s][0] + values[s][1]
            if q % 3 == 0 and 16 * (q // 3) < NCOEF:
                rows = slice(16 * (q // 3), min(16 * (q // 3) + 16, NCOEF))
                for o in blocks:
                    m2m_high[o, rows], m2m_low[o, rows] = halves(m2m[o, rows])
        return carry

    lax.fori_loop(0, 4, two_blocks, 0)
    for first in range(0, NCOEF, 8):
        rows = [sums[pl.ds(8 * first + r, 8, stride=8), :] for r in range(8)]
        check[first : first + 8] = ((rows[0] + rows[1]) + (rows[2] + rows[3])) + ((rows[4] + rows[5]) + (rows[6] + rows[7]))
    potentials = jnp.transpose(check[...])[:, :NCOEF]
    potentials = potentials[:LEAF_DEV] + potentials[LEAF_DEV:]
    leaf_density = product(potentials, uc2ue_high[...], uc2ue_low[...])
    rounded = shrunk(two_bf16(leaf_density), shrink_parts[...]).astype(bf16)
    row = lax.broadcasted_iota(jnp.int32, (32, 128), 0)
    col = lax.broadcasted_iota(jnp.int32, (32, 128), 1)
    odd = (col >> 6) * 4 + (row >> 2 & 1) * 2 + (row & 1)
    parent = (row >> 4) * 4 + (row >> 3 & 1) * 2 + (row >> 1 & 1)
    order = jnp.where(col & (LEAF_DEV - 1) == odd * 8 + parent, 1.0, 0.0).astype(bf16)
    nothing = jnp.zeros((LEAF_DEV, RANK), bf16)
    pairs = jnp.concatenate(
        [jnp.concatenate([rounded, nothing], axis=1), jnp.concatenate([nothing, rounded], axis=1)], axis=0
    )
    block_ref[0:32] = jnp.dot(order, pairs, preferred_element_type=f32).astype(bf16)

    pl.semaphore_wait(barrier, peers - 1)
    for number in near_numbers:
        near_copy(number, 0).start()
    nearby[1, own, 0:32] = block_ref[0:32]

    mid_density = jnp.zeros((8, NCOEF), f32)
    for o in range(8):
        mid_density += product(leaf_density[8 * o : 8 * o + 8], m2m_high[o], m2m_low[o])
    shrink = shrink_parts[...]
    mid_pairs = shrunk(two_bf16(mid_density), shrink)
    mid_pairs = jnp.concatenate([mid_pairs[:4], mid_pairs[4:]], axis=1)
    block_ref[32:48] = jnp.concatenate([mid_pairs, jnp.zeros((12, 2 * RANK), f32)], axis=0).astype(bf16)
    for number in near_numbers:
        near_copy(number, 1).start()
    nearby[1, own, 32:48] = block_ref[32:48]

    load(4).wait()
    directions = stored_ref.shape[2]

    def turn(j, carry):
        pairs = jnp.concatenate([stored_ref[j], stored_ref[j + HALF]], axis=0)
        operator_rows[pl.ds(j, directions, stride=PITCH), :] = jnp.transpose(pairs).astype(f32)
        return carry

    for j in range(HALF):
        turn(j, 0)
    lift = shrunk(jnp.concatenate([m2m_high[octant], m2m_low[octant]], axis=0), shrink)
    own_density = jnp.zeros((8, NCOEF), f32)
    for o in range(8):
        child = jnp.broadcast_to(mid_density[o : o + 1], (8, NCOEF))
        own_density += product(child, m2m_high[o], m2m_low[o])
    lifted = product(own_density, *halves(lift))
    own_multipole = shrunk(two_bf16(own_density), shrink).astype(bf16).astype(f32)
    small_ref[...] = jnp.concatenate([own_multipole[:1], lifted[:1]], axis=1)

    def send_small(k, carry):
        small_copy(k).start()
        return carry

    lax.fori_loop(1, peers, send_small, 0, unroll=peers - 1 if peers <= 64 else 5)
    every[pl.ds(me, 1)] = small_ref[...]

    row = lax.broadcasted_iota(jnp.int32, (224, 256), 0)
    col = lax.broadcasted_iota(jnp.int32, (224, 256), 1)
    step_y = (row >> 5) - 3
    slot = ((row >> 4) & 1) * 4 + (col >> 6)
    step_z = jnp.where(slot < 4, slot - 3 + 3 * (slot >> 1), slot - 5)
    usable = slot < 7

    def chosen(side_bits, target, source, step, bit):
        target = (bit << side_bits) + target
        return (source - target == step) & (jnp.abs((source >> 1) - (target >> 1)) <= 1)

    leaf_select = (
        usable
        & chosen(2, (row >> 2) & 3, (((col >> 5) & 1) << 2) + ((col >> 2) & 3), step_y, y_bit)
        & chosen(2, row & 3, (((col >> 4) & 1) << 2) + (col & 3), step_z, z_bit)
    )
    leaf_select = jnp.where(leaf_select, 1.0, 0.0).astype(bf16)
    mid_base = (
        usable
        & ((row & 15) < 4)
        & ((col & 15) < 4)
        & chosen(1, (row >> 1) & 1, (((col >> 5) & 1) << 1) + ((col >> 1) & 1), step_y, y_bit)
        & chosen(1, row & 1, (((col >> 4) & 1) << 1) + (col & 1), step_z, z_bit)
    )
    mid_select = jnp.where(mid_base, 1.0, 0.0).astype(bf16)
    on_diagonal = (lax.broadcasted_iota(jnp.int32, (256, 256), 0) >> 6) == (
        (lax.broadcasted_iota(jnp.int32, (256, 256), 1) >> 5) & 3
    )

    blank = jnp.zeros((14, 16, 256), bf16)
    leaf_rows[0] = blank
    leaf_rows[9] = blank
    mid_rows[0] = blank
    mid_rows[7] = blank

    blank = jnp.zeros((14, 16, 256), bf16)
    leaf_rows[0] = blank
    leaf_rows[9] = blank
    mid_rows[0] = blank
    mid_rows[7] = blank
    for c in range(3):
        near_whole(c, 0).wait_recv()
        near_whole(c, 1).wait_recv()

    for c in range(3):
        inside = (column + c >= 1) & (column + c <= columns_x)
        diagonal = jnp.where(on_diagonal & inside, 1.0, 0.0).astype(bf16)
        for first in range(0, 48, 16):
            if (c, first) in ((0, 0), (2, 16)):
                continue
            stack = nearby[c, :, first : first + 16, :].reshape(64, 128)
            for lx in range(2):
                low = stack[:, RANK * lx : RANK * lx + HALF]
                high = stack[:, RANK * lx + HALF : RANK * lx + RANK]
                wide = jnp.concatenate([low] * 4 + [high] * 4, axis=1)
                sources = jnp.concatenate([wide] * 4, axis=0) * diagonal
                if first == 32:
                    got = jnp.dot(mid_select, sources, preferred_element_type=f32)
                    mid_rows[2 * c + lx + 1] = got.astype(bf16).reshape(14, 16, 256)
                else:
                    got = jnp.dot(leaf_select, sources, preferred_element_type=f32)
                    leaf_rows[4 * c + first // 8 + lx - 1] = got.astype(bf16).reshape(14, 16, 256)

    bases = {-3: 0, -2: 49, 2: 218, 3: 267}
    first_direction = 0
    odd_target = (lax.broadcasted_iota(jnp.int32, (192, 128), 0) >> 4) & 1
    total = jnp.zeros((192, 128), f32)
    for u in range(7):
        part = jnp.zeros((192, 128), f32)
        for v in range(7):

            def operand(quads):
                rows = []
                for lanes in (slice(0, 128), slice(128, 256)):
                    for ref, count in ((leaf_rows, 4), (mid_rows, 2)):
                        pieces = [
                            ref[u : u + count, 2 * v + quad, :, lanes].reshape(16 * count, 128)
                            for quad in quads
                        ]
                        rows.append(jnp.concatenate(pieces, axis=1))
                return jnp.concatenate(rows, axis=0)

            def operators(steps):
                rows = [operator_rows[(first_direction + k) * PITCH : (first_direction + k) * PITCH + HALF] for k in steps]
                return jnp.concatenate(rows, axis=0).astype(bf16)

            if 2 <= u <= 4 and 2 <= v <= 4:
                part += jnp.dot(operand((0,)), operators((0, 1, 2, 3)), preferred_element_type=f32)
                first_direction += 4
            else:
                part += jnp.dot(operand((0, 1)), operators((0, 1, 5, 6, 2, 3, 4, 4)), preferred_element_type=f32)
                first_direction += 7
        if u == 0:
            part = jnp.where(odd_target == 1, part, 0.0)
        if u == 6:
            part = jnp.where(odd_target == 0, part, 0.0)
        total += part
    total = total[:96, :RANK] + total[96:, RANK:]
    packed_ref[1:5] = total[64:68]
    packed_ref[5:9] = total[80:84]
    packed_ref[9:73] = total[:64]

    small_whole().wait_recv()
    own_total = jnp.zeros((1, RANK), f32)
    for u in (-3, -2, 2, 3):
        other = column + u
        good = (other >= 0) & (other < columns_x)
        if u == -3:
            good = good & (column % 2 == 1)
        if u == 3:
            good = good & (column % 2 == 0)
        wrapped = (other + 4 * columns_x) % columns_x
        part = jnp.zeros((1, RANK), f32)
        for sy in range(2):
            for sz in range(2):
                direction = bases[u] + (sy - y_bit + 3) * 7 + (sz - z_bit + 3)
                source = every[pl.ds(wrapped * 4 + sy * 2 + sz, 1)].astype(bf16)
                rows = pl.ds(pl.multiple_of(direction * PITCH, 8), HALF)
                operator = operator_rows[rows].astype(bf16)
                part += jnp.dot(source[:, :HALF], operator[:, :RANK], preferred_element_type=f32)
                part += jnp.dot(source[:, HALF:RANK], operator[:, RANK:], preferred_element_type=f32)
        own_total += jnp.where(good, part, 0.0)
    packed_ref[0:1] = own_total

    load(5).wait()
    padded[...] = jnp.zeros_like(padded)
    for r in range(root_count):
        padded[root_count + r : root_count + r + 1] = jnp.sum(every[8 * r : 8 * r + 8], axis=0, keepdims=True)
    found = jnp.zeros((root_count, RANK), f32)
    for k in range(2 * root_count - 1):
        distance = k - (root_count - 1)
        if abs(distance) >= 2:
            start = root_count + distance
            source = padded[start : start + root_count, :][:, RANK:].astype(bf16)
            found += jnp.dot(source, root_ref[k], preferred_element_type=f32)
    packed_ref[FIRST_ROOT : FIRST_ROOT + root_count] = found

    for c in range(3):
        near_whole(c, 0).wait_send()
        near_whole(c, 1).wait_send()
    small_whole().wait_send()


def finish_kernel(packed_ref, boxes_ref, roots_ref):
    boxes_ref[...] = jnp.transpose(packed_ref[...])[:, : LEAF_DEV + 9]
    roots_ref[...] = packed_ref[FIRST_ROOT : FIRST_ROOT + roots_ref.shape[0]]


def body(offsets, forces, counts, uc2ue, m2m_ops, compress, m2l_ops, root_ops):
    f32, bf16 = jnp.float32, jnp.bfloat16
    peers = lax.axis_size("morton")
    root_count = peers // 8
    vmem, anywhere = pl.BlockSpec(memory_space=pltpu.VMEM), pl.BlockSpec(memory_space=pl.ANY)
    stored = jnp.transpose(m2l_ops, (1, 2, 0))
    directions = m2l_ops.shape[0]
    packed = pl.pallas_call(
        functools.partial(solver_kernel, peers),
        out_shape=pltpu.VMEM((FIRST_ROOT + (root_count + 7) // 8 * 8, RANK), f32),
        in_specs=[pl.BlockSpec(memory_space=pltpu.SMEM)] + [anywhere] * 7,
        out_specs=vmem,
        scratch_shapes=[
            pltpu.VMEM(offsets.shape, f32),
            pltpu.VMEM(forces.shape, f32),
            pltpu.VMEM(uc2ue.shape, f32),
            pltpu.VMEM((RANK, NCOEF), f32),
            pltpu.VMEM(uc2ue.shape, bf16),
            pltpu.VMEM(uc2ue.shape, bf16),
            pltpu.VMEM((2 * RANK, NCOEF), bf16),
            pltpu.VMEM(m2m_ops.shape, f32),
            pltpu.VMEM(m2m_ops.shape, bf16),
            pltpu.VMEM(m2m_ops.shape, bf16),
            pltpu.VMEM(stored.shape, bf16),
            pltpu.VMEM(root_ops.shape, bf16),
            pltpu.VMEM((512, 128), f32),
            pltpu.VMEM((6 * LEAF_PITCH, P_CAP), f32),
            pltpu.VMEM((8, FORCE + 6, 8, 128), f32),
            pltpu.VMEM((8 * NCOEF, 128), f32),
            pltpu.VMEM((1, 128), f32),
            pltpu.VMEM((48, 128), bf16),
            pltpu.VMEM((peers, 128), f32),
            pltpu.VMEM((3, 4, 48, 128), bf16),
            pltpu.VMEM((10, 14, 16, 256), bf16),
            pltpu.VMEM((8, 14, 16, 256), bf16),
            pltpu.VMEM((directions * PITCH, 2 * RANK), f32),
            pltpu.VMEM((3 * root_count, 128), f32),
            pltpu.SemaphoreType.DMA((6,)),
            pltpu.SemaphoreType.DMA((8,)),
            pltpu.SemaphoreType.DMA,
            pltpu.SemaphoreType.DMA,
            pltpu.SemaphoreType.DMA((2, 3)),
            pltpu.SemaphoreType.DMA((2, 3)),
        ],
        compiler_params=pltpu.CompilerParams(collective_id=0, has_side_effects=True, vmem_limit_bytes=60 << 20),
    )(counts, offsets, forces, uc2ue, compress.T, m2m_ops, stored, root_ops)
    boxes, roots = pl.pallas_call(
        finish_kernel,
        out_shape=(
            jax.ShapeDtypeStruct((RANK, LEAF_DEV + 9), f32),
            jax.ShapeDtypeStruct((root_count, RANK), f32),
        ),
        in_specs=[vmem],
        out_specs=(vmem, vmem),
        compiler_params=pltpu.CompilerParams(vmem_limit_bytes=1 << 20),
    )(packed)
    return jnp.transpose(boxes), roots


def solution(mesh):
    placed = (P(None, "morton"), P(None, "morton"), P("morton"), P(), P(), P(), P(), P())
    return jax.shard_map(
        body, mesh=mesh, in_specs=placed, out_specs=(P("morton", None), P()), check_vma=False
    )
```

```python
import functools

import jax
import jax.numpy as jnp
import numpy as np
from jax import lax
from jax.experimental import pallas as pl
from jax.experimental.pallas import tpu as pltpu
from jax.sharding import PartitionSpec as P

SURF_ORDER = 6
NCOEF = 456
RANK = 64
P_CAP = 128
LEAF_DEV = 64
HALF = RANK // 2
PITCH = HALF + 8
FIRST_ROOT = (LEAF_DEV + 9 + 7) // 8 * 8


check_radius = 1.475
LEAF_PITCH = LEAF_DEV + 8
APART = tuple(3 * SURF_ORDER * s for s in range(3))
SQUARE = tuple(first + SURF_ORDER for first in APART)
ALONG = tuple(first + 2 * SURF_ORDER for first in APART)
FORCE = 9 * SURF_ORDER
MESH = pl.DeviceIdType.MESH


def surface_grid():
    order = range(SURF_ORDER)
    ends = (0, SURF_ORDER - 1)
    surface = [(i, j, k) for i in order for j in order for k in order if i in ends or j in ends or k in ends]
    return surface, [float(np.float32(check_radius * tick)) for tick in np.linspace(-1.0, 1.0, SURF_ORDER)]


def two_parts(value):
    high = value.astype(jnp.bfloat16).astype(jnp.float32)
    return high, value - high


def product(value, high, low):
    rows = value.shape[0]
    parts = two_bf16(value)
    both = jnp.dot(parts, low, preferred_element_type=jnp.float32)
    both += jnp.dot(parts, high, preferred_element_type=jnp.float32)
    return both[:rows] + both[rows:]


def two_bf16(value):
    return jnp.concatenate(two_parts(value), axis=0).astype(jnp.bfloat16)


def shrunk(parts, shrink):
    dims = (((1,), (1,)), ((), ()))
    both = lax.dot_general(parts, shrink, dims, preferred_element_type=jnp.float32)
    rows, rank = parts.shape[0] // 2, shrink.shape[0] // 2
    both = both[:rows] + both[rows:]
    return both[:, :rank] + both[:, rank:]


def halves(matrix):
    high, low = two_parts(matrix)
    return high.astype(jnp.bfloat16), low.astype(jnp.bfloat16)


def solver_kernel(peers, counts_ref, offsets_hbm, forces_hbm, uc2ue_hbm, compress_hbm, m2m_hbm, stored_hbm, root_hbm,
                  packed_ref,
                  offsets_ref, forces_ref, uc2ue_ref, compress_ref, m2m, m2m_high, m2m_low, stored_ref, root_ref, check,
                  slots_by_leaf, table, sums,
                  small_ref, block_ref, every, nearby, leaf_rows, mid_rows, operator_rows, padded,
                  loads, arrivals, send_all, recv_all, send_near, recv_near):
    f32, bf16 = jnp.float32, jnp.bfloat16
    surface, ticks = surface_grid()
    points = len(surface)
    me = lax.axis_index("morton")
    columns_x, root_count = peers // 4, peers // 8
    column, y_bit, z_bit = me // 4, me // 2 % 2, me % 2
    own, octant = me % 4, me % 8

    wholes = (
        (offsets_hbm, offsets_ref),
        (forces_hbm, forces_ref),
        (uc2ue_hbm, uc2ue_ref),
        (compress_hbm, compress_ref),
        (stored_hbm, stored_ref),
        (root_hbm, root_ref),
    )

    def load(number):
        return pltpu.make_async_copy(*wholes[number], loads.at[number])

    for number in range(4):
        load(number).start()
    for o in range(8):
        pltpu.make_async_copy(m2m_hbm.at[o], m2m.at[o], arrivals.at[o]).start()
    load(4).start()
    load(5).start()

    def around(k):
        return jnp.where(me + k >= peers, me + k - peers, me + k)

    barrier = pltpu.get_barrier_semaphore()

    def greet(k, carry):
        pl.semaphore_signal(barrier, inc=1, device_id=(around(k),), device_id_type=MESH)
        return carry

    lax.fori_loop(1, peers, greet, 0, unroll=4)

    parts = {-1: (0, 32), 0: (0, 48), 1: (16, 48)}

    def near_copy(number):
        dc, flip_y, flip_z = number // 4 - 1, number // 2 % 2, number % 2
        other = (y_bit + flip_y) % 2 * 2 + (z_bit + flip_z) % 2
        peer = (column + dc + columns_x) % columns_x * 4 + other
        first, last = parts[dc]
        return pltpu.make_async_remote_copy(
            src_ref=block_ref.at[first:last],
            dst_ref=nearby.at[1 - dc, own, first:last],
            send_sem=send_near.at[1 - dc], recv_sem=recv_near.at[1 - dc],
            device_id=(peer,), device_id_type=MESH)

    def near_whole(c):
        count, (first, last) = (3 if c == 1 else 4), parts[1 - c]
        space = nearby.at[c, 0:count, first:last]
        return pltpu.make_async_remote_copy(
            src_ref=space, dst_ref=space, send_sem=send_near.at[c], recv_sem=recv_near.at[c],
            device_id=(me,), device_id_type=MESH)

    def small_copy(k):
        return pltpu.make_async_remote_copy(
            src_ref=small_ref, dst_ref=every.at[pl.ds(me, 1)], send_sem=send_all, recv_sem=recv_all,
            device_id=(around(k),), device_id_type=MESH)

    def small_whole():
        space = every.at[0 : peers - 1]
        return pltpu.make_async_remote_copy(
            src_ref=space, dst_ref=space, send_sem=send_all, recv_sem=recv_all,
            device_id=(me,), device_id_type=MESH)

    sums[...] = jnp.zeros_like(sums)
    check[NCOEF:] = jnp.zeros((check.shape[0] - NCOEF, 128), f32)
    load(0).wait()
    load(1).wait()
    lane_row = lax.broadcasted_iota(jnp.int32, (1, P_CAP), 1)

    def place(leaf, carry):
        odd = (leaf >> 4 & 1) * 4 + (leaf >> 2 & 1) * 2 + (leaf & 1)
        parent = (leaf >> 5 & 1) * 4 + (leaf >> 3 & 1) * 2 + (leaf >> 1 & 1)
        slots = pl.ds(pl.multiple_of(leaf * P_CAP, P_CAP), P_CAP)
        live = lane_row < counts_ref[leaf]
        slots_by_leaf[pl.ds(odd * 8 + parent, 3, stride=LEAF_PITCH), :] = offsets_ref[:, slots]
        slots_by_leaf[pl.ds(3 * LEAF_PITCH + odd * 8 + parent, 3, stride=LEAF_PITCH), :] = jnp.where(
            live, forces_ref[:, slots], 0.0
        )
        return carry

    lax.fori_loop(0, LEAF_DEV, place, 0, unroll=16)
    for s in range(6):
        leaves = slots_by_leaf[s * LEAF_PITCH : s * LEAF_PITCH + LEAF_DEV]
        leaves = jnp.concatenate([leaves[:, : P_CAP // 2], leaves[:, P_CAP // 2 :]], axis=0)
        table[:, FORCE + 3 + s if s < 3 else FORCE + s - 3] = jnp.transpose(leaves).reshape(8, 8, 128)

    for block in range(8):
        for s in range(3):
            place, force = table[block, FORCE + 3 + s], table[block, FORCE + s]
            for i in range(SURF_ORDER):
                apart = ticks[i] - place
                table[block, APART[s] + i] = apart
                table[block, SQUARE[s] + i] = apart * apart
                table[block, ALONG[s] + i] = apart * force

    def two_blocks(step, carry):
        blocks = (2 * step, 2 * step + 1)
        for o in blocks:
            pltpu.make_async_copy(m2m_hbm.at[o], m2m.at[o], arrivals.at[o]).wait()
        force = [[table[block, FORCE + s] for s in range(3)] for block in blocks]
        column_now = None
        for q, (i, j, k) in enumerate(surface):
            if (i, j) != column_now:
                column_now = (i, j)
                square = [table[block, SQUARE[0] + i] + table[block, SQUARE[1] + j] for block in blocks]
                along = [table[block, ALONG[0] + i] + table[block, ALONG[1] + j] for block in blocks]
            values = [[], [], []]
            for n, block in enumerate(blocks):
                inverse = lax.rsqrt(square[n] + table[block, SQUARE[2] + k])
                projected = along[n] + table[block, ALONG[2] + k]
                scaled = projected * (inverse * inverse)
                for s, tick in enumerate((i, j, k)):
                    values[s].append((force[n][s] + table[block, APART[s] + tick] * scaled) * inverse)
            for s in range(3):
                rows = slice((s * points + q) * 8, (s * points + q) * 8 + 8)
                sums[rows] += values[s][0] + values[s][1]
            if q % 3 == 0 and 16 * (q // 3) < NCOEF:
                rows = slice(16 * (q // 3), min(16 * (q // 3) + 16, NCOEF))
                for o in blocks:
                    m2m_high[o, rows], m2m_low[o, rows] = halves(m2m[o, rows])
        return carry

    lax.fori_loop(0, 4, two_blocks, 0)
    for first in range(0, NCOEF, 8):
        rows = [sums[pl.ds(8 * first + r, 8, stride=8), :] for r in range(8)]
        check[first : first + 8] = ((rows[0] + rows[1]) + (rows[2] + rows[3])) + ((rows[4] + rows[5]) + (rows[6] + rows[7]))
    potentials = jnp.transpose(check[...])[:, :NCOEF]
    potentials = potentials[:LEAF_DEV] + potentials[LEAF_DEV:]
    load(2).wait()
    load(3).wait()
    leaf_density = product(potentials, *halves(uc2ue_ref[...]))
    shrink = jnp.concatenate(halves(compress_ref[...]), axis=0)
    rounded = shrunk(two_bf16(leaf_density), shrink).astype(bf16)
    mid_density = jnp.zeros((8, NCOEF), f32)
    for o in range(8):
        mid_density += product(leaf_density[8 * o : 8 * o + 8], m2m_high[o], m2m_low[o])
    row = lax.broadcasted_iota(jnp.int32, (32, 128), 0)
    col = lax.broadcasted_iota(jnp.int32, (32, 128), 1)
    odd = (col >> 6) * 4 + (row >> 2 & 1) * 2 + (row & 1)
    parent = (row >> 4) * 4 + (row >> 3 & 1) * 2 + (row >> 1 & 1)
    order = jnp.where((col & (LEAF_DEV - 1)) == odd * 8 + parent, 1.0, 0.0).astype(bf16)
    nothing = jnp.zeros((LEAF_DEV, RANK), bf16)
    pairs = jnp.concatenate(
        [jnp.concatenate([rounded, nothing], axis=1), jnp.concatenate([nothing, rounded], axis=1)], axis=0
    )
    leaves = jnp.dot(order, pairs, preferred_element_type=f32).astype(bf16)
    block_ref[0:16] = leaves[:16]
    block_ref[32:48] = leaves[16:]
    mid_pairs = shrunk(two_bf16(mid_density), shrink)
    mid_pairs = jnp.concatenate([mid_pairs[:4], mid_pairs[4:]], axis=1)
    block_ref[16:32] = jnp.concatenate([mid_pairs, jnp.zeros((12, 2 * RANK), f32)], axis=0).astype(bf16)

    pl.semaphore_wait(barrier, peers - 1)
    near_numbers = [number for number in range(12) if number != 4]
    for number in near_numbers:
        near_copy(number).start()
    nearby[1, own] = block_ref[...]

    load(4).wait()
    directions = stored_ref.shape[2]

    def turn(j, carry):
        pairs = jnp.concatenate([stored_ref[j], stored_ref[j + HALF]], axis=0)
        operator_rows[pl.ds(j, directions, stride=PITCH), :] = jnp.transpose(pairs).astype(f32)
        return carry

    for j in range(HALF):
        turn(j, 0)
    lift = shrunk(jnp.concatenate([m2m_high[octant], m2m_low[octant]], axis=0), shrink)
    own_density = jnp.zeros((8, NCOEF), f32)
    for o in range(8):
        child = jnp.broadcast_to(mid_density[o : o + 1], (8, NCOEF))
        own_density += product(child, m2m_high[o], m2m_low[o])
    lifted = product(own_density, *halves(lift))
    own_multipole = shrunk(two_bf16(own_density), shrink).astype(bf16).astype(f32)
    small_ref[...] = jnp.concatenate([own_multipole[:1], lifted[:1]], axis=1)

    def send_small(k, carry):
        small_copy(k).start()
        return carry

    lax.fori_loop(1, peers, send_small, 0, unroll=4)
    every[pl.ds(me, 1)] = small_ref[...]

    row = lax.broadcasted_iota(jnp.int32, (224, 256), 0)
    col = lax.broadcasted_iota(jnp.int32, (224, 256), 1)
    step_y = (row >> 5) - 3
    slot = ((row >> 4) & 1) * 4 + (col >> 6)
    step_z = jnp.where(slot < 4, slot - 3 + 3 * (slot >> 1), slot - 5)
    usable = slot < 7

    def chosen(side_bits, target, source, step, bit):
        target = (bit << side_bits) + target
        return (source - target == step) & (jnp.abs((source >> 1) - (target >> 1)) <= 1)

    leaf_select = (
        usable
        & chosen(2, (row >> 2) & 3, (((col >> 5) & 1) << 2) + ((col >> 2) & 3), step_y, y_bit)
        & chosen(2, row & 3, (((col >> 4) & 1) << 2) + (col & 3), step_z, z_bit)
    )
    leaf_select = jnp.where(leaf_select, 1.0, 0.0).astype(bf16)
    mid_base = (
        usable
        & ((row & 15) < 4)
        & ((col & 15) < 4)
        & chosen(1, (row >> 1) & 1, (((col >> 5) & 1) << 1) + ((col >> 1) & 1), step_y, y_bit)
        & chosen(1, row & 1, (((col >> 4) & 1) << 1) + (col & 1), step_z, z_bit)
    )
    mid_select = jnp.where(mid_base, 1.0, 0.0).astype(bf16)
    on_diagonal = (lax.broadcasted_iota(jnp.int32, (256, 256), 0) >> 6) == (
        (lax.broadcasted_iota(jnp.int32, (256, 256), 1) >> 5) & 3
    )

    blank = jnp.zeros((14, 16, 256), bf16)
    leaf_rows[0] = blank
    leaf_rows[9] = blank
    mid_rows[0] = blank
    mid_rows[7] = blank

    blank = jnp.zeros((14, 16, 256), bf16)
    leaf_rows[0] = blank
    leaf_rows[9] = blank
    mid_rows[0] = blank
    mid_rows[7] = blank
    for c in range(3):
        near_whole(c).wait_recv()

    for c in range(3):
        inside = (column + c >= 1) & (column + c <= columns_x)
        diagonal = jnp.where(on_diagonal & inside, 1.0, 0.0).astype(bf16)
        for first in range(0, 48, 16):
            if (c, first) in ((0, 0), (2, 32)):
                continue
            stack = nearby[c, :, first : first + 16, :].reshape(64, 128)
            for lx in range(2):
                low = stack[:, RANK * lx : RANK * lx + HALF]
                high = stack[:, RANK * lx + HALF : RANK * lx + RANK]
                wide = jnp.concatenate([low] * 4 + [high] * 4, axis=1)
                sources = jnp.concatenate([wide] * 4, axis=0) * diagonal
                if first == 16:
                    got = jnp.dot(mid_select, sources, preferred_element_type=f32)
                    mid_rows[2 * c + lx + 1] = got.astype(bf16).reshape(14, 16, 256)
                else:
                    got = jnp.dot(leaf_select, sources, preferred_element_type=f32)
                    leaf_rows[4 * c + first // 16 + lx - 1] = got.astype(bf16).reshape(14, 16, 256)

    bases = {-3: 0, -2: 49, 2: 218, 3: 267}
    first_direction = 0
    odd_target = (lax.broadcasted_iota(jnp.int32, (192, 128), 0) >> 4) & 1
    total = jnp.zeros((192, 128), f32)
    for u in range(7):
        part = jnp.zeros((192, 128), f32)
        for v in range(7):

            def operand(quads):
                rows = []
                for lanes in (slice(0, 128), slice(128, 256)):
                    for ref, count in ((leaf_rows, 4), (mid_rows, 2)):
                        pieces = [
                            ref[u : u + count, 2 * v + quad, :, lanes].reshape(16 * count, 128)
                            for quad in quads
                        ]
                        rows.append(jnp.concatenate(pieces, axis=1))
                return jnp.concatenate(rows, axis=0)

            def operators(steps):
                rows = [operator_rows[(first_direction + k) * PITCH : (first_direction + k) * PITCH + HALF] for k in steps]
                return jnp.concatenate(rows, axis=0).astype(bf16)

            if 2 <= u <= 4 and 2 <= v <= 4:
                part += jnp.dot(operand((0,)), operators((0, 1, 2, 3)), preferred_element_type=f32)
                first_direction += 4
            else:
                part += jnp.dot(operand((0, 1)), operators((0, 1, 5, 6, 2, 3, 4, 4)), preferred_element_type=f32)
                first_direction += 7
        if u == 0:
            part = jnp.where(odd_target == 1, part, 0.0)
        if u == 6:
            part = jnp.where(odd_target == 0, part, 0.0)
        total += part
    total = total[:96, :RANK] + total[96:, RANK:]
    packed_ref[1:5] = total[64:68]
    packed_ref[5:9] = total[80:84]
    packed_ref[9:73] = total[:64]

    small_whole().wait_recv()
    own_total = jnp.zeros((1, RANK), f32)
    for u in (-3, -2, 2, 3):
        other = column + u
        good = (other >= 0) & (other < columns_x)
        if u == -3:
            good = good & (column % 2 == 1)
        if u == 3:
            good = good & (column % 2 == 0)
        wrapped = (other + 4 * columns_x) % columns_x
        part = jnp.zeros((1, RANK), f32)
        for sy in range(2):
            for sz in range(2):
                direction = bases[u] + (sy - y_bit + 3) * 7 + (sz - z_bit + 3)
                source = every[pl.ds(wrapped * 4 + sy * 2 + sz, 1)].astype(bf16)
                rows = pl.ds(pl.multiple_of(direction * PITCH, 8), HALF)
                operator = operator_rows[rows].astype(bf16)
                part += jnp.dot(source[:, :HALF], operator[:, :RANK], preferred_element_type=f32)
                part += jnp.dot(source[:, HALF:RANK], operator[:, RANK:], preferred_element_type=f32)
        own_total += jnp.where(good, part, 0.0)
    packed_ref[0:1] = own_total

    load(5).wait()
    padded[...] = jnp.zeros_like(padded)
    for r in range(root_count):
        padded[root_count + r : root_count + r + 1] = jnp.sum(every[8 * r : 8 * r + 8], axis=0, keepdims=True)
    found = jnp.zeros((root_count, RANK), f32)
    for k in range(2 * root_count - 1):
        distance = k - (root_count - 1)
        if abs(distance) >= 2:
            start = root_count + distance
            source = padded[start : start + root_count, :][:, RANK:].astype(bf16)
            found += jnp.dot(source, root_ref[k], preferred_element_type=f32)
    packed_ref[FIRST_ROOT : FIRST_ROOT + root_count] = found

    for c in range(3):
        near_whole(c).wait_send()
    small_whole().wait_send()


def finish_kernel(packed_ref, boxes_ref, roots_ref):
    boxes_ref[...] = jnp.transpose(packed_ref[...])[:, : LEAF_DEV + 9]
    roots_ref[...] = packed_ref[FIRST_ROOT : FIRST_ROOT + roots_ref.shape[0]]


def body(offsets, forces, counts, uc2ue, m2m_ops, compress, m2l_ops, root_ops):
    f32, bf16 = jnp.float32, jnp.bfloat16
    peers = lax.axis_size("morton")
    root_count = peers // 8
    vmem, anywhere = pl.BlockSpec(memory_space=pltpu.VMEM), pl.BlockSpec(memory_space=pl.ANY)
    stored = jnp.transpose(m2l_ops, (1, 2, 0))
    directions = m2l_ops.shape[0]
    packed = pl.pallas_call(
        functools.partial(solver_kernel, peers),
        out_shape=pltpu.VMEM((FIRST_ROOT + (root_count + 7) // 8 * 8, RANK), f32),
        in_specs=[pl.BlockSpec(memory_space=pltpu.SMEM)] + [anywhere] * 7,
        out_specs=vmem,
        scratch_shapes=[
            pltpu.VMEM(offsets.shape, f32),
            pltpu.VMEM(forces.shape, f32),
            pltpu.VMEM(uc2ue.shape, f32),
            pltpu.VMEM((RANK, NCOEF), f32),
            pltpu.VMEM(m2m_ops.shape, f32),
            pltpu.VMEM(m2m_ops.shape, bf16),
            pltpu.VMEM(m2m_ops.shape, bf16),
            pltpu.VMEM(stored.shape, bf16),
            pltpu.VMEM(root_ops.shape, bf16),
            pltpu.VMEM((512, 128), f32),
            pltpu.VMEM((6 * LEAF_PITCH, P_CAP), f32),
            pltpu.VMEM((8, FORCE + 6, 8, 128), f32),
            pltpu.VMEM((8 * NCOEF, 128), f32),
            pltpu.VMEM((1, 128), f32),
            pltpu.VMEM((48, 128), bf16),
            pltpu.VMEM((peers, 128), f32),
            pltpu.VMEM((3, 4, 48, 128), bf16),
            pltpu.VMEM((10, 14, 16, 256), bf16),
            pltpu.VMEM((8, 14, 16, 256), bf16),
            pltpu.VMEM((directions * PITCH, 2 * RANK), f32),
            pltpu.VMEM((3 * root_count, 128), f32),
            pltpu.SemaphoreType.DMA((6,)),
            pltpu.SemaphoreType.DMA((8,)),
            pltpu.SemaphoreType.DMA,
            pltpu.SemaphoreType.DMA,
            pltpu.SemaphoreType.DMA((3,)),
            pltpu.SemaphoreType.DMA((3,)),
        ],
        compiler_params=pltpu.CompilerParams(collective_id=0, has_side_effects=True, vmem_limit_bytes=60 << 20),
    )(counts, offsets, forces, uc2ue, compress.T, m2m_ops, stored, root_ops)
    boxes, roots = pl.pallas_call(
        finish_kernel,
        out_shape=(
            jax.ShapeDtypeStruct((RANK, LEAF_DEV + 9), f32),
            jax.ShapeDtypeStruct((root_count, RANK), f32),
        ),
        in_specs=[vmem],
        out_specs=(vmem, vmem),
        compiler_params=pltpu.CompilerParams(vmem_limit_bytes=1 << 20),
    )(packed)
    return jnp.transpose(boxes), roots


def solution(mesh):
    placed = (P(None, "morton"), P(None, "morton"), P("morton"), P(), P(), P(), P(), P())
    return jax.shard_map(
        body, mesh=mesh, in_specs=placed, out_specs=(P("morton", None), P()), check_vma=False
    )
```

```python
import functools

import jax
import jax.numpy as jnp
import numpy as np
from jax import lax
from jax.experimental import pallas as pl
from jax.experimental.pallas import tpu as pltpu
from jax.sharding import PartitionSpec as P

SURF_ORDER = 6
NCOEF = 456
RANK = 64
P_CAP = 128
LEAF_DEV = 64
HALF = RANK // 2
PITCH = HALF + 8
FIRST_ROOT = (LEAF_DEV + 9 + 7) // 8 * 8


check_radius = 1.475
LEAF_PITCH = LEAF_DEV + 8
APART = tuple(3 * SURF_ORDER * s for s in range(3))
SQUARE = tuple(first + SURF_ORDER for first in APART)
ALONG = tuple(first + 2 * SURF_ORDER for first in APART)
FORCE = 9 * SURF_ORDER
MESH = pl.DeviceIdType.MESH


def surface_grid():
    order = range(SURF_ORDER)
    ends = (0, SURF_ORDER - 1)
    surface = [(i, j, k) for i in order for j in order for k in order if i in ends or j in ends or k in ends]
    return surface, [float(np.float32(check_radius * tick)) for tick in np.linspace(-1.0, 1.0, SURF_ORDER)]


def two_parts(value):
    high = value.astype(jnp.bfloat16).astype(jnp.float32)
    return high, value - high


def product(value, high, low):
    rows = value.shape[0]
    parts = two_bf16(value)
    both = jnp.dot(parts, low, preferred_element_type=jnp.float32)
    both += jnp.dot(parts, high, preferred_element_type=jnp.float32)
    return both[:rows] + both[rows:]


def two_bf16(value):
    return jnp.concatenate(two_parts(value), axis=0).astype(jnp.bfloat16)


def shrunk(parts, shrink):
    dims = (((1,), (1,)), ((), ()))
    both = lax.dot_general(parts, shrink, dims, preferred_element_type=jnp.float32)
    rows, rank = parts.shape[0] // 2, shrink.shape[0] // 2
    both = both[:rows] + both[rows:]
    return both[:, :rank] + both[:, rank:]


def halves(matrix):
    high, low = two_parts(matrix)
    return high.astype(jnp.bfloat16), low.astype(jnp.bfloat16)


def solver_kernel(peers, counts_ref, offsets_hbm, forces_hbm, uc2ue_hbm, compress_hbm, m2m_hbm, stored_hbm, root_hbm,
                  packed_ref,
                  offsets_ref, forces_ref, uc2ue_ref, compress_ref, m2m, m2m_high, m2m_low, stored_ref, root_ref, check,
                  slots_by_leaf, table, sums,
                  small_ref, block_ref, every, nearby, leaf_rows, mid_rows, operator_rows, padded,
                  loads, arrivals, send_all, recv_all, send_near, recv_near):
    f32, bf16 = jnp.float32, jnp.bfloat16
    surface, ticks = surface_grid()
    points = len(surface)
    me = lax.axis_index("morton")
    columns_x, root_count = peers // 4, peers // 8
    column, y_bit, z_bit = me // 4, me // 2 % 2, me % 2
    own, octant = me % 4, me % 8

    wholes = (
        (offsets_hbm, offsets_ref),
        (forces_hbm, forces_ref),
        (uc2ue_hbm, uc2ue_ref),
        (compress_hbm, compress_ref),
        (stored_hbm, stored_ref),
        (root_hbm, root_ref),
    )

    def load(number):
        return pltpu.make_async_copy(*wholes[number], loads.at[number])

    for number in range(4):
        load(number).start()
    for o in range(8):
        pltpu.make_async_copy(m2m_hbm.at[o], m2m.at[o], arrivals.at[o]).start()
    load(4).start()
    load(5).start()

    def around(k):
        return jnp.where(me + k >= peers, me + k - peers, me + k)

    barrier = pltpu.get_barrier_semaphore()

    def greet(k, carry):
        pl.semaphore_signal(barrier, inc=1, device_id=(around(k),), device_id_type=MESH)
        return carry

    lax.fori_loop(1, peers, greet, 0, unroll=4)

    parts = {-1: (0, 32), 0: (0, 48), 1: (16, 48)}

    def near_copy(number):
        dc, flip_y, flip_z = number // 4 - 1, number // 2 % 2, number % 2
        other = (y_bit + flip_y) % 2 * 2 + (z_bit + flip_z) % 2
        peer = (column + dc + columns_x) % columns_x * 4 + other
        first, last = parts[dc]
        return pltpu.make_async_remote_copy(
            src_ref=block_ref.at[first:last],
            dst_ref=nearby.at[1 - dc, own, first:last],
            send_sem=send_near.at[1 - dc], recv_sem=recv_near.at[1 - dc],
            device_id=(peer,), device_id_type=MESH)

    def near_whole(c):
        count, (first, last) = (3 if c == 1 else 4), parts[1 - c]
        space = nearby.at[c, 0:count, first:last]
        return pltpu.make_async_remote_copy(
            src_ref=space, dst_ref=space, send_sem=send_near.at[c], recv_sem=recv_near.at[c],
            device_id=(me,), device_id_type=MESH)

    def small_copy(k):
        return pltpu.make_async_remote_copy(
            src_ref=small_ref, dst_ref=every.at[pl.ds(me, 1)], send_sem=send_all, recv_sem=recv_all,
            device_id=(around(k),), device_id_type=MESH)

    def small_whole():
        space = every.at[0 : peers - 1]
        return pltpu.make_async_remote_copy(
            src_ref=space, dst_ref=space, send_sem=send_all, recv_sem=recv_all,
            device_id=(me,), device_id_type=MESH)

    sums[...] = jnp.zeros_like(sums)
    check[NCOEF:] = jnp.zeros((check.shape[0] - NCOEF, 128), f32)
    load(0).wait()
    load(1).wait()
    lane_row = lax.broadcasted_iota(jnp.int32, (1, P_CAP), 1)

    def place(leaf, carry):
        odd = (leaf >> 4 & 1) * 4 + (leaf >> 2 & 1) * 2 + (leaf & 1)
        parent = (leaf >> 5 & 1) * 4 + (leaf >> 3 & 1) * 2 + (leaf >> 1 & 1)
        slots = pl.ds(pl.multiple_of(leaf * P_CAP, P_CAP), P_CAP)
        live = lane_row < counts_ref[leaf]
        slots_by_leaf[pl.ds(odd * 8 + parent, 3, stride=LEAF_PITCH), :] = offsets_ref[:, slots]
        slots_by_leaf[pl.ds(3 * LEAF_PITCH + odd * 8 + parent, 3, stride=LEAF_PITCH), :] = jnp.where(
            live, forces_ref[:, slots], 0.0
        )
        return carry

    lax.fori_loop(0, LEAF_DEV, place, 0, unroll=16)
    for s in range(6):
        leaves = slots_by_leaf[s * LEAF_PITCH : s * LEAF_PITCH + LEAF_DEV]
        leaves = jnp.concatenate([leaves[:, : P_CAP // 2], leaves[:, P_CAP // 2 :]], axis=0)
        table[:, FORCE + 3 + s if s < 3 else FORCE + s - 3] = jnp.transpose(leaves).reshape(8, 8, 128)

    for block in range(8):
        for s in range(3):
            place, force = table[block, FORCE + 3 + s], table[block, FORCE + s]
            for i in range(SURF_ORDER):
                apart = ticks[i] - place
                table[block, APART[s] + i] = apart
                table[block, SQUARE[s] + i] = apart * apart
                table[block, ALONG[s] + i] = apart * force

    def two_blocks(step, carry):
        blocks = (2 * step, 2 * step + 1)
        for o in blocks:
            pltpu.make_async_copy(m2m_hbm.at[o], m2m.at[o], arrivals.at[o]).wait()
        force = [[table[block, FORCE + s] for s in range(3)] for block in blocks]
        column_now = None
        for q, (i, j, k) in enumerate(surface):
            if (i, j) != column_now:
                column_now = (i, j)
                square = [table[block, SQUARE[0] + i] + table[block, SQUARE[1] + j] for block in blocks]
                along = [table[block, ALONG[0] + i] + table[block, ALONG[1] + j] for block in blocks]
            values = [[], [], []]
            for n, block in enumerate(blocks):
                inverse = lax.rsqrt(square[n] + table[block, SQUARE[2] + k])
                projected = along[n] + table[block, ALONG[2] + k]
                scaled = projected * (inverse * inverse)
                for s, tick in enumerate((i, j, k)):
                    values[s].append((force[n][s] + table[block, APART[s] + tick] * scaled) * inverse)
            for s in range(3):
                rows = slice((s * points + q) * 8, (s * points + q) * 8 + 8)
                sums[rows] += values[s][0] + values[s][1]
            if q % 3 == 0 and 16 * (q // 3) < NCOEF:
                rows = slice(16 * (q // 3), min(16 * (q // 3) + 16, NCOEF))
                for o in blocks:
                    m2m_high[o, rows], m2m_low[o, rows] = halves(m2m[o, rows])
        return carry

    lax.fori_loop(0, 4, two_blocks, 0)
    for first in range(0, NCOEF, 8):
        rows = [sums[pl.ds(8 * first + r, 8, stride=8), :] for r in range(8)]
        check[first : first + 8] = ((rows[0] + rows[1]) + (rows[2] + rows[3])) + ((rows[4] + rows[5]) + (rows[6] + rows[7]))
    potentials = jnp.transpose(check[...])[:, :NCOEF]
    potentials = potentials[:LEAF_DEV] + potentials[LEAF_DEV:]
    load(2).wait()
    load(3).wait()
    leaf_density = product(potentials, *halves(uc2ue_ref[...]))
    shrink = jnp.concatenate(halves(compress_ref[...]), axis=0)
    rounded = shrunk(two_bf16(leaf_density), shrink).astype(bf16)
    mid_density = jnp.zeros((8, NCOEF), f32)
    for o in range(8):
        mid_density += product(leaf_density[8 * o : 8 * o + 8], m2m_high[o], m2m_low[o])
    row = lax.broadcasted_iota(jnp.int32, (32, 128), 0)
    col = lax.broadcasted_iota(jnp.int32, (32, 128), 1)
    odd = (col >> 6) * 4 + (row >> 2 & 1) * 2 + (row & 1)
    parent = (row >> 4) * 4 + (row >> 3 & 1) * 2 + (row >> 1 & 1)
    order = jnp.where((col & (LEAF_DEV - 1)) == odd * 8 + parent, 1.0, 0.0).astype(bf16)
    nothing = jnp.zeros((LEAF_DEV, RANK), bf16)
    pairs = jnp.concatenate(
        [jnp.concatenate([rounded, nothing], axis=1), jnp.concatenate([nothing, rounded], axis=1)], axis=0
    )
    leaves = jnp.dot(order, pairs, preferred_element_type=f32).astype(bf16)
    block_ref[0:16] = leaves[:16]
    block_ref[32:48] = leaves[16:]
    mid_pairs = shrunk(two_bf16(mid_density), shrink)
    mid_pairs = jnp.concatenate([mid_pairs[:4], mid_pairs[4:]], axis=1)
    block_ref[16:32] = jnp.concatenate([mid_pairs, jnp.zeros((12, 2 * RANK), f32)], axis=0).astype(bf16)

    pl.semaphore_wait(barrier, peers - 1)
    near_numbers = [number for number in range(12) if number != 4]
    for number in near_numbers:
        near_copy(number).start()
    nearby[1, own] = block_ref[...]

    load(4).wait()
    directions = stored_ref.shape[2]

    def turn(j, carry):
        pairs = jnp.concatenate([stored_ref[j], stored_ref[j + HALF]], axis=0)
        operator_rows[pl.ds(j, directions, stride=PITCH), :] = jnp.transpose(pairs).astype(f32)
        return carry

    for j in range(HALF):
        turn(j, 0)
    lift = shrunk(jnp.concatenate([m2m_high[octant], m2m_low[octant]], axis=0), shrink)
    own_density = jnp.zeros((8, NCOEF), f32)
    for o in range(8):
        child = jnp.broadcast_to(mid_density[o : o + 1], (8, NCOEF))
        own_density += product(child, m2m_high[o], m2m_low[o])
    lifted = product(own_density, *halves(lift))
    own_multipole = shrunk(two_bf16(own_density), shrink).astype(bf16).astype(f32)
    small_ref[...] = jnp.concatenate([own_multipole[:1], lifted[:1]], axis=1)

    def send_small(k, carry):
        small_copy(k).start()
        return carry

    lax.fori_loop(1, peers, send_small, 0, unroll=4)
    every[pl.ds(me, 1)] = small_ref[...]

    row = lax.broadcasted_iota(jnp.int32, (224, 256), 0)
    col = lax.broadcasted_iota(jnp.int32, (224, 256), 1)
    step_y = (row >> 5) - 3
    slot = ((row >> 4) & 1) * 4 + (col >> 6)
    step_z = jnp.where(slot < 4, slot - 3 + 3 * (slot >> 1), slot - 5)
    usable = slot < 7

    def chosen(side_bits, target, source, step, bit):
        target = (bit << side_bits) + target
        return (source - target == step) & (jnp.abs((source >> 1) - (target >> 1)) <= 1)

    leaf_select = (
        usable
        & chosen(2, (row >> 2) & 3, (((col >> 5) & 1) << 2) + ((col >> 2) & 3), step_y, y_bit)
        & chosen(2, row & 3, (((col >> 4) & 1) << 2) + (col & 3), step_z, z_bit)
    )
    leaf_select = jnp.where(leaf_select, 1.0, 0.0).astype(bf16)
    mid_base = (
        usable
        & ((row & 15) < 4)
        & ((col & 15) < 4)
        & chosen(1, (row >> 1) & 1, (((col >> 5) & 1) << 1) + ((col >> 1) & 1), step_y, y_bit)
        & chosen(1, row & 1, (((col >> 4) & 1) << 1) + (col & 1), step_z, z_bit)
    )
    mid_select = jnp.where(mid_base, 1.0, 0.0).astype(bf16)
    on_diagonal = (lax.broadcasted_iota(jnp.int32, (256, 256), 0) >> 6) == (
        (lax.broadcasted_iota(jnp.int32, (256, 256), 1) >> 5) & 3
    )

    blank = jnp.zeros((14, 16, 256), bf16)
    leaf_rows[0] = blank
    leaf_rows[9] = blank
    mid_rows[0] = blank
    mid_rows[7] = blank

    blank = jnp.zeros((14, 16, 256), bf16)
    leaf_rows[0] = blank
    leaf_rows[9] = blank
    mid_rows[0] = blank
    mid_rows[7] = blank
    for c in range(3):
        near_whole(c).wait_recv()

    for c in range(3):
        inside = (column + c >= 1) & (column + c <= columns_x)
        diagonal = jnp.where(on_diagonal & inside, 1.0, 0.0).astype(bf16)
        for first in range(0, 48, 16):
            if (c, first) in ((0, 0), (2, 32)):
                continue
            stack = nearby[c, :, first : first + 16, :].reshape(64, 128)
            for lx in range(2):
                low = stack[:, RANK * lx : RANK * lx + HALF]
                high = stack[:, RANK * lx + HALF : RANK * lx + RANK]
                wide = jnp.concatenate([low] * 4 + [high] * 4, axis=1)
                sources = jnp.concatenate([wide] * 4, axis=0) * diagonal
                if first == 16:
                    got = jnp.dot(mid_select, sources, preferred_element_type=f32)
                    mid_rows[2 * c + lx + 1] = got.astype(bf16).reshape(14, 16, 256)
                else:
                    got = jnp.dot(leaf_select, sources, preferred_element_type=f32)
                    leaf_rows[4 * c + first // 16 + lx - 1] = got.astype(bf16).reshape(14, 16, 256)

    bases = {-3: 0, -2: 49, 2: 218, 3: 267}
    first_direction = 0
    odd_target = (lax.broadcasted_iota(jnp.int32, (192, 128), 0) >> 4) & 1
    total = jnp.zeros((192, 128), f32)
    for u in range(7):
        part = jnp.zeros((192, 128), f32)
        for v in range(7):

            def operand(quads):
                rows = []
                for lanes in (slice(0, 128), slice(128, 256)):
                    for ref, count in ((leaf_rows, 4), (mid_rows, 2)):
                        pieces = [
                            ref[u : u + count, 2 * v + quad, :, lanes].reshape(16 * count, 128)
                            for quad in quads
                        ]
                        rows.append(jnp.concatenate(pieces, axis=1))
                return jnp.concatenate(rows, axis=0)

            def operators(steps):
                rows = [operator_rows[(first_direction + k) * PITCH : (first_direction + k) * PITCH + HALF] for k in steps]
                return jnp.concatenate(rows, axis=0).astype(bf16)

            if 2 <= u <= 4 and 2 <= v <= 4:
                part += jnp.dot(operand((0,)), operators((0, 1, 2, 3)), preferred_element_type=f32)
                first_direction += 4
            else:
                part += jnp.dot(operand((0, 1)), operators((0, 1, 5, 6, 2, 3, 4, 4)), preferred_element_type=f32)
                first_direction += 7
        if u == 0:
            part = jnp.where(odd_target == 1, part, 0.0)
        if u == 6:
            part = jnp.where(odd_target == 0, part, 0.0)
        total += part
    total = total[:96, :RANK] + total[96:, RANK:]
    packed_ref[1:5] = total[64:68]
    packed_ref[5:9] = total[80:84]
    packed_ref[9:73] = total[:64]

    for c in range(3):
        near_whole(c).wait_send()
    small_whole().wait_send()
    load(5).wait()
    small_whole().wait_recv()
    own_total = jnp.zeros((1, RANK), f32)
    for u in (-3, -2, 2, 3):
        other = column + u
        good = (other >= 0) & (other < columns_x)
        if u == -3:
            good = good & (column % 2 == 1)
        if u == 3:
            good = good & (column % 2 == 0)
        wrapped = (other + 4 * columns_x) % columns_x
        part = jnp.zeros((1, RANK), f32)
        for sy in range(2):
            for sz in range(2):
                direction = bases[u] + (sy - y_bit + 3) * 7 + (sz - z_bit + 3)
                source = every[pl.ds(wrapped * 4 + sy * 2 + sz, 1)].astype(bf16)
                rows = pl.ds(pl.multiple_of(direction * PITCH, 8), HALF)
                operator = operator_rows[rows].astype(bf16)
                part += jnp.dot(source[:, :HALF], operator[:, :RANK], preferred_element_type=f32)
                part += jnp.dot(source[:, HALF:RANK], operator[:, RANK:], preferred_element_type=f32)
        own_total += jnp.where(good, part, 0.0)
    packed_ref[0:1] = own_total

    gathered = jnp.sum(every[...].reshape(root_count, 8, 2 * RANK), axis=1)[:, RANK:]
    padded[0:root_count] = jnp.zeros((root_count, RANK), f32)
    padded[root_count : 2 * root_count] = gathered
    padded[2 * root_count :] = jnp.zeros((root_count, RANK), f32)
    found = jnp.zeros((root_count, RANK), f32)
    for k in range(2 * root_count - 1):
        distance = k - (root_count - 1)
        if abs(distance) >= 2:
            start = root_count + distance
            source = padded[start : start + root_count].astype(bf16)
            found += jnp.dot(source, root_ref[k], preferred_element_type=f32)
    packed_ref[FIRST_ROOT : FIRST_ROOT + root_count] = found


def finish_kernel(packed_ref, boxes_ref, roots_ref):
    boxes_ref[...] = jnp.transpose(packed_ref[...])[:, : LEAF_DEV + 9]
    roots_ref[...] = packed_ref[FIRST_ROOT : FIRST_ROOT + roots_ref.shape[0]]


def body(offsets, forces, counts, uc2ue, m2m_ops, compress, m2l_ops, root_ops):
    f32, bf16 = jnp.float32, jnp.bfloat16
    peers = lax.axis_size("morton")
    root_count = peers // 8
    vmem, anywhere = pl.BlockSpec(memory_space=pltpu.VMEM), pl.BlockSpec(memory_space=pl.ANY)
    stored = jnp.transpose(m2l_ops, (1, 2, 0))
    directions = m2l_ops.shape[0]
    packed = pl.pallas_call(
        functools.partial(solver_kernel, peers),
        out_shape=pltpu.VMEM((FIRST_ROOT + (root_count + 7) // 8 * 8, RANK), f32),
        in_specs=[pl.BlockSpec(memory_space=pltpu.SMEM)] + [anywhere] * 7,
        out_specs=vmem,
        scratch_shapes=[
            pltpu.VMEM(offsets.shape, f32),
            pltpu.VMEM(forces.shape, f32),
            pltpu.VMEM(uc2ue.shape, f32),
            pltpu.VMEM((RANK, NCOEF), f32),
            pltpu.VMEM(m2m_ops.shape, f32),
            pltpu.VMEM(m2m_ops.shape, bf16),
            pltpu.VMEM(m2m_ops.shape, bf16),
            pltpu.VMEM(stored.shape, bf16),
            pltpu.VMEM(root_ops.shape, bf16),
            pltpu.VMEM((512, 128), f32),
            pltpu.VMEM((6 * LEAF_PITCH, P_CAP), f32),
            pltpu.VMEM((8, FORCE + 6, 8, 128), f32),
            pltpu.VMEM((8 * NCOEF, 128), f32),
            pltpu.VMEM((1, 128), f32),
            pltpu.VMEM((48, 128), bf16),
            pltpu.VMEM((peers, 128), f32),
            pltpu.VMEM((3, 4, 48, 128), bf16),
            pltpu.VMEM((10, 14, 16, 256), bf16),
            pltpu.VMEM((8, 14, 16, 256), bf16),
            pltpu.VMEM((directions * PITCH, 2 * RANK), f32),
            pltpu.VMEM((3 * root_count, RANK), f32),
            pltpu.SemaphoreType.DMA((6,)),
            pltpu.SemaphoreType.DMA((8,)),
            pltpu.SemaphoreType.DMA,
            pltpu.SemaphoreType.DMA,
            pltpu.SemaphoreType.DMA((3,)),
            pltpu.SemaphoreType.DMA((3,)),
        ],
        compiler_params=pltpu.CompilerParams(collective_id=0, has_side_effects=True, vmem_limit_bytes=60 << 20),
    )(counts, offsets, forces, uc2ue, compress.T, m2m_ops, stored, root_ops)
    boxes, roots = pl.pallas_call(
        finish_kernel,
        out_shape=(
            jax.ShapeDtypeStruct((RANK, LEAF_DEV + 9), f32),
            jax.ShapeDtypeStruct((root_count, RANK), f32),
        ),
        in_specs=[vmem],
        out_specs=(vmem, vmem),
        compiler_params=pltpu.CompilerParams(vmem_limit_bytes=1 << 20),
    )(packed)
    return jnp.transpose(boxes), roots


def solution(mesh):
    placed = (P(None, "morton"), P(None, "morton"), P("morton"), P(), P(), P(), P(), P())
    return jax.shard_map(
        body, mesh=mesh, in_specs=placed, out_specs=(P("morton", None), P()), check_vma=False
    )
```
